32 devices in a mesh: track: 4 (over y, x), tm: 8 (over z, core).
Axes of the slice: x: 2, y: 2, z: 4, core: 2. Of those that a mesh axis runs over, the one named last changes fastest.
Arguments:
- observations: float32 [1024, 16, 128], P('tm', 'track'), may hold values from -18 to 18
- dynamics: bfloat16 [256, 128, 128], P('track'), may hold values from -1 to 1
- smoother_gain: bfloat16 [256, 128, 128], P('track'), may hold values from -1 to 1
- gains: bfloat16 [256, 128], P('track'), may hold values from 0 to 1
- regime: int32 [256], P('tm'), may hold values from 0 to 255
Outputs:
- smoothed: float32 [1024, 16, 128], P('tm', 'track')
The draws below stay inside these ranges and needn't reach their ends.
All inputs are finite; a program needn't handle non-finite values.
Results may differ from the reference program's by a relative error of at most 0.0003.
Values may be sent and summed in bfloat16 or wider, within the bound.
No kernel may reach another device: no remote copies, remote signals or barrier semaphores. Data moves between devices by JAX's collectives and lax.ppermute only.
A program may use at most 64 MiB of HBM per device.

```python
import jax
import jax.numpy as jnp
from jax import lax

N = 128
REGIMES = 256
DWELL = 4
STEPS = 1024
TRACKS = 16
BLOCKS = 256


def orthogonal_set(key):
    normal_mat = jax.random.normal(key, (REGIMES, N, N), jnp.float32)
    q_mat, r_mat = jnp.linalg.qr(normal_mat)
    signs = jnp.sign(jnp.diagonal(r_mat, axis1=1, axis2=2))
    return q_mat * signs[:, None, :]


def draw_dynamics(key, part):
    first_key, second_key = jax.random.split(jax.random.fold_in(key, 11))
    rotation = orthogonal_set(first_key)
    scales = jax.random.uniform(second_key, (REGIMES, N), jnp.float32, 1.0 - 1.6 / STEPS, 1.0)
    return (scales[:, :, None] * rotation).astype(jnp.bfloat16)


def draw_smoother_gain(key, part):
    first_key, second_key = jax.random.split(jax.random.fold_in(key, 23))
    rotation = orthogonal_set(first_key)
    scales = jax.random.uniform(second_key, (REGIMES, N), jnp.float32, 1.0 - 2.4 / STEPS, 1.0)
    return (scales[:, :, None] * rotation).astype(jnp.bfloat16)


def draw_gains(key, part):
    lowest = jnp.log(0.16 / STEPS)
    highest = jnp.log(3.2 / STEPS)
    spread = jax.random.uniform(jax.random.fold_in(key, 37), (REGIMES, N), jnp.float32, 0.0, 1.0)
    values = jnp.exp(lowest + (highest - lowest) * spread)
    return values.astype(jnp.bfloat16)


def plant(values, rng, least, high):
    spot = [jax.random.randint(jax.random.fold_in(rng, axis), (), 0, length) for axis, length in enumerate(values.shape)]
    main_axis = values.shape.index(max(values.shape))
    next_to = spot[:main_axis] + [(spot[main_axis] + 1) % values.shape[main_axis]] + spot[main_axis + 1:]
    return values.at[tuple(spot)].set(least).at[tuple(next_to)].set(high)


def shard_levels(key, extent, cuts, smallest, top_value):
    gain = 1.0
    for axis_at, parts in cuts:
        heights = jax.random.uniform(jax.random.fold_in(jax.random.fold_in(key, 6), axis_at), (parts,), jnp.float32, smallest / len(cuts), top_value / len(cuts))
        gain = gain * jnp.repeat(jnp.exp(heights), extent[axis_at] // parts).reshape((-1,) + (1,) * (len(extent) - 1 - axis_at))
    return gain


def centred(stream_key, shape, deviation, bound, cuts=(), dtype=jnp.bfloat16):
    drawn = jax.random.normal(stream_key, shape, jnp.float32) * deviation
    if len(cuts) > 0:
        drawn = shard_levels(stream_key, shape, cuts, -0.22, 0.18) * drawn
    return jnp.clip(drawn, min=-bound, max=bound).astype(dtype)


def setup_inputs(seed: int = 0) -> dict:
    arg_keys = jax.random.split(jax.random.key(seed), 6)
    return {
        "observations": centred(arg_keys[0], (STEPS, TRACKS, N), 3.0, 18.0, ((0, 8), (1, 4)), jnp.float32),
        "dynamics": draw_dynamics(jax.random.fold_in(arg_keys[5], 71), 0),
        "smoother_gain": draw_smoother_gain(jax.random.fold_in(arg_keys[5], 71), 0),
        "gains": draw_gains(jax.random.fold_in(arg_keys[5], 71), 0),
        "regime": plant(jax.random.randint(arg_keys[4], (BLOCKS,), 0, REGIMES), jax.random.fold_in(arg_keys[4], 1), 0, REGIMES - 1).astype(jnp.int32),
    }


def matmul(left, right):
    return jnp.dot(left, right, precision=lax.Precision.HIGHEST)

def reference(observations, dynamics, smoother_gain, gains, regime):
    step_ids = jnp.repeat(regime, DWELL).astype(jnp.int32)
    next_ids = jnp.concatenate([step_ids[1:], jnp.zeros((1,), jnp.int32)])
    live = (jnp.arange(STEPS) < STEPS - 1).astype(jnp.float32)

    def forward(state, inputs):
        measured, which = inputs
        trans = dynamics[which].astype(jnp.float32)
        gain_vec = gains[which].astype(jnp.float32)
        closed = (1.0 - gain_vec)[:, None] * trans
        state = matmul(state, closed.T) + gain_vec[None, :] * measured
        return (state, state)
    start = jnp.zeros((TRACKS, N), jnp.float32)
    _, filtered = lax.scan(forward, start, (observations, step_ids))

    def backward(after, inputs):
        current, which, keep = inputs
        trans = dynamics[which].astype(jnp.float32)
        gain_mat = smoother_gain[which].astype(jnp.float32) * keep
        cross = matmul(gain_mat, trans)
        value = current - matmul(current, cross.T) + matmul(after, gain_mat.T)
        return (value, value)
    _, smoothed = lax.scan(backward, start, (filtered, next_ids, live), reverse=True)
    return smoothed
```

```python
import functools

import jax
import jax.numpy as jnp
from jax import lax
from jax.experimental import pallas as pl
from jax.experimental.pallas import tpu as pltpu
from jax.sharding import PartitionSpec as P


F32 = jnp.float32
BF16 = jnp.bfloat16
VMEM = pl.BlockSpec(memory_space=pltpu.VMEM)
SMEM = pl.BlockSpec(memory_space=pltpu.SMEM)
ANY = pl.BlockSpec(memory_space=pl.ANY)
STRANDS = 4


def xor_pairs(axis, mask):
    count = lax.axis_size(axis)
    return [(source, source ^ mask) for source in range(count)]


def call(kernel, outs, ins, cost, scratch=()):
    return pl.pallas_call(
        kernel,
        out_shape=outs,
        in_specs=ins,
        out_specs=[VMEM] * len(outs),
        scratch_shapes=list(scratch),
        cost_estimate=pl.CostEstimate(flops=cost, bytes_accessed=cost // 64, transcendentals=0),
    )


def shape(dims, dtype=F32):
    return jax.ShapeDtypeStruct(dims, dtype)


def split(value):
    high = value.astype(BF16)
    low = (value - high.astype(F32)).astype(BF16)
    return high, low


def times_rows(value, doubled):
    pieces = jnp.concatenate(split(value), axis=1)
    return lax.dot_general(
        pieces, doubled, (((1,), (1,)), ((), ())), preferred_element_type=F32
    )


def times(value, matrix):
    high, low = split(value)
    upper, lower = split(matrix)
    left = jnp.concatenate([high, low, high], axis=1)
    right = jnp.concatenate([upper, upper, lower], axis=0)
    return jnp.dot(left, right, preferred_element_type=F32)


def compose(earlier, later, width):
    product = times(earlier, later[:width])
    return jnp.concatenate([product[:width], product[width:] + later[width:]], axis=0)


def place_of():
    return lax.axis_index("track")


def choose(index, options):
    value = options[0]
    for j in range(1, len(options)):
        value = jnp.where(index == j, options[j], value)
    return value


def measured_kernel(groups, share, span, regime_ref, gains_ref, obs_ref, *refs):
    outs, table = (refs[:groups], refs[groups])
    me = place_of()
    owned = gains_ref.shape[0]
    table[...] = gains_ref[...].astype(F32)
    tracks, width = obs_ref.shape[1:]
    for j in range(groups):
        peer = me ^ j
        first = pl.multiple_of(peer * span, span)
        outs[j][0:span] = obs_ref[pl.ds(first, span)]
        for b in range(share):
            at = jnp.clip(regime_ref[peer * share + b] - me * owned, 0, owned - 1)
            outs[j][span + b] = jnp.broadcast_to(table[pl.ds(at, 1), :], (tracks, width))


def gather_kernel(groups, share, regime_ref, table_ref, *refs):
    outs, sems = (refs[:groups], refs[groups])
    me = place_of()
    owned = table_ref.shape[0]
    for j in range(groups):
        peer = me ^ j
        for b in range(share):
            at = jnp.clip(regime_ref[peer * share + b] - me * owned, 0, owned - 1)
            pltpu.make_async_copy(table_ref.at[at], outs[j].at[b], sems.at[j]).start()
    for j in range(groups):
        pltpu.make_async_copy(table_ref.at[pl.ds(0, share)], outs[j], sems.at[j]).wait()


def pick_matrix(regime_ref, share, owned, me, parts, b):
    source = (regime_ref[me * share + b] // owned) ^ me
    return choose(source, [part[b] for part in parts])


def doubled(matrix):
    return jnp.concatenate([matrix, matrix], axis=1)


def gain_rows(regime_ref, share, owned, me, span, parts, b):
    source = (regime_ref[me * share + b] // owned) ^ me
    return choose(source, [part[span + b][0:1] for part in parts])


def step_rows(parts, t):
    return jnp.concatenate([part[t] for part in parts], axis=0)


def forward_kernel(groups, share, span, owned, regime_ref, *refs):
    mats, meas = (refs[:groups], refs[groups : 2 * groups])
    total_ref, strand_ref, picked_ref = refs[2 * groups :]
    me = place_of()
    width = mats[0].shape[1]
    rows = groups * meas[0].shape[1]
    dwell = span // share
    per = share // STRANDS
    weights, gains = ([], [])
    for b in range(share):
        picked = pick_matrix(regime_ref, share, owned, me, mats, b)
        picked_ref[b] = picked
        weights.append(doubled(picked))
        gains.append(gain_rows(regime_ref, share, owned, me, span, meas, b))
    unit = (
        lax.broadcasted_iota(jnp.int32, (width, width), 0)
        == lax.broadcasted_iota(jnp.int32, (width, width), 1)
    ).astype(F32)
    start = jnp.concatenate([unit, jnp.zeros((rows, width), F32)], axis=0)
    states = [start] * STRANDS
    for i in range(per * dwell):
        for s in range(STRANDS):
            b = s * per + i // dwell
            t = b * dwell + i % dwell
            moved = times_rows(states[s], weights[b])
            kept = moved * (1.0 - gains[b])
            driven = gains[b] * step_rows(meas, t)
            states[s] = jnp.concatenate([kept[:width], kept[width:] + driven], axis=0)
    for s in range(STRANDS):
        strand_ref[s] = states[s]
    while len(states) > 1:
        states = [compose(states[i], states[i + 1], width) for i in range(0, len(states), 2)]
    total_ref[...] = states[0]


def backward_kernel(groups, share, span, owned, regime_ref, *refs):
    mats = refs[:groups]
    total_ref, strand_ref, picked_ref = refs[groups:]
    me = place_of()
    width = mats[0].shape[1]
    dwell = span // share
    per = share // STRANDS
    weights = []
    for b in range(share):
        picked = pick_matrix(regime_ref, share, owned, me, mats, b)
        picked_ref[b] = picked
        weights.append(doubled(picked))
    unit = (
        lax.broadcasted_iota(jnp.int32, (width, width), 0)
        == lax.broadcasted_iota(jnp.int32, (width, width), 1)
    ).astype(F32)
    states = [unit] * STRANDS
    for i in range(per * dwell):
        for s in range(STRANDS):
            b = s * per + per - 1 - i // dwell
            states[s] = times_rows(states[s], weights[b])
    for s in range(STRANDS):
        strand_ref[s] = states[s]
    while len(states) > 1:
        states = [times(states[i + 1], states[i]) for i in range(0, len(states), 2)]
    total_ref[...] = states[0]


def swapped(rows, mask, groups):
    block = rows.shape[0] // groups
    return jnp.concatenate(
        [rows[(j ^ mask) * block : ((j ^ mask) + 1) * block] for j in range(groups)], axis=0
    )


def is_later(axis, mask):
    return (lax.axis_index(axis) & mask) != 0


def join_kernel(axis, mask, groups, reverse, own_ref, other_ref, joined_ref, fixed_ref):
    width = own_ref.shape[1]
    own, other = (own_ref[...], other_ref[...])
    if axis == "track":
        other = jnp.concatenate([other[:width], swapped(other[width:], mask, groups)], axis=0)
    fixed_ref[...] = other
    swap = is_later(axis, mask)
    if reverse:
        swap = jnp.logical_not(swap)
    joined_ref[...] = compose(jnp.where(swap, other, own), jnp.where(swap, own, other), width)


def carried(levels, parts, top, reverse):
    width = parts[0].shape[1]
    axis, mask = levels[-1]
    goes = is_later(axis, mask)
    if reverse:
        goes = jnp.logical_not(goes)
    carry = jnp.where(goes, top, jnp.zeros_like(top))
    for (axis, mask), part in zip(levels[-2::-1], parts[::-1]):
        goes = is_later(axis, mask)
        if reverse:
            goes = jnp.logical_not(goes)
        carry = jnp.where(goes, times(carry, part[:width]) + part[width:], carry)
    return carry


def filter_kernel(levels, groups, share, span, owned, regime_ref, *refs):
    count = len(levels) - 1
    parts = refs[:count]
    top_ref, fstrand_ref, bstrand_ref, fpick_ref, bpick_ref = refs[count : count + 5]
    meas = refs[count + 5 : count + 5 + groups]
    filtered_ref, pushed_ref, out_ref, bmap_ref, total_ref = refs[count + 5 + groups :]
    me = place_of()
    width = fpick_ref.shape[1]
    rows = top_ref.shape[0]
    dwell = span // share
    per = share // STRANDS
    carry = carried(levels, [part[...] for part in parts], top_ref[...], False)
    starts = [carry]
    for s in range(STRANDS - 1):
        strand = fstrand_ref[s]
        starts.append(times(starts[-1], strand[:width]) + strand[width:])
    gains = [gain_rows(regime_ref, share, owned, me, span, meas, b) for b in range(share)]
    weights = [doubled(fpick_ref[b]) for b in range(share)]
    states = starts
    pushes = [None] * span
    for i in range(per * dwell):
        for s in range(STRANDS):
            b = s * per + i // dwell
            t = b * dwell + i % dwell
            ahead = times_rows(states[s], weights[b])
            pushes[t] = gains[b] * (step_rows(meas, t) - ahead)
            states[s] = ahead + pushes[t]
            filtered_ref[t] = states[s]
            pushed_ref[t] = pushes[t]
    weights = [doubled(bpick_ref[b]) for b in range(share)]
    states = [None] * STRANDS
    for i in range(per * dwell):
        for s in range(STRANDS):
            b = s * per + per - 1 - i // dwell
            t = b * dwell + dwell - 1 - i % dwell
            state = pushes[t] if i == 0 else states[s] + pushes[t]
            states[s] = times_rows(state, weights[b])
    state = states[-1]
    for s in range(STRANDS - 2, -1, -1):
        state = times(state, bstrand_ref[s]) + states[s]
    for s in range(STRANDS):
        out_ref[s] = states[s]
    total_ref[0:width] = bmap_ref[...]
    total_ref[width:] = state


def smooth_kernel(levels, groups, share, span, *refs):
    count = len(levels) - 1
    parts = refs[:count]
    top_ref, bstrand_ref, bpick_ref, filtered_ref, pushed_ref, zero_ref = refs[count : count + 6]
    outs = refs[count + 6 :]
    dwell = span // share
    per = share // STRANDS
    tracks = outs[0].shape[1]
    carry = carried(levels, [part[...] for part in parts], top_ref[...], True)
    starts = [carry]
    for s in range(STRANDS - 1, 0, -1):
        starts.append(times(starts[-1], bstrand_ref[s]) + zero_ref[s])
    states = starts[::-1]
    weights = [doubled(bpick_ref[b]) for b in range(share)]
    for i in range(per * dwell):
        for s in range(STRANDS):
            b = s * per + per - 1 - i // dwell
            t = b * dwell + dwell - 1 - i % dwell
            value = filtered_ref[t] + states[s]
            for j in range(groups):
                outs[j][t] = value[j * tracks : (j + 1) * tracks]
            if i < per * dwell - 1:
                states[s] = times_rows(states[s] + pushed_ref[t], weights[b])


def collect_kernel(groups, span, *refs):
    parts, out_ref = (refs[:groups], refs[groups])
    me = place_of()
    for j in range(groups):
        first = pl.multiple_of((me ^ j) * span, span)
        out_ref[pl.ds(first, span)] = parts[j][...]


def body(observations, dynamics, smoother_gain, gains, regime):
    length, tracks, width = observations.shape
    blocks = regime.shape[0]
    groups = lax.axis_size("track")
    dwell = length // blocks
    share = blocks // groups
    span = share * dwell
    owned = dynamics.shape[0]
    rows = groups * tracks
    levels = []
    for axis in ("track", "tm"):
        mask = 1
        while mask < lax.axis_size(axis):
            levels.append((axis, mask))
            mask *= 2
    big = width * width * width

    def exchange(values):
        return [values[0]] + [
            lax.ppermute(values[j], "track", xor_pairs("track", j)) for j in range(1, groups)
        ]

    meas = call(
        functools.partial(measured_kernel, groups, share, span),
        [shape((span + share, tracks, width))] * groups,
        [SMEM, VMEM, VMEM],
        big,
        [pltpu.VMEM((owned, width), F32)],
    )(regime, gains, observations)
    meas = exchange(meas)

    def gathered(table):
        return call(
            functools.partial(gather_kernel, groups, share),
            [shape((share, width, width), BF16)] * groups,
            [SMEM, ANY],
            4 * big,
            [pltpu.SemaphoreType.DMA((groups,))],
        )(regime, table)

    trans = exchange(gathered(dynamics))
    smooth = exchange(gathered(smoother_gain))

    total, fstrand, fpick = call(
        functools.partial(forward_kernel, groups, share, span, owned),
        [shape((width + rows, width)), shape((STRANDS, width + rows, width)),
         shape((share, width, width), BF16)],
        [SMEM] + [VMEM] * (2 * groups),
        400 * big,
    )(regime, *trans, *meas)

    def scan_levels(total, reverse):
        parts = []
        for axis, mask in levels[:-1]:
            other = lax.ppermute(total, axis, xor_pairs(axis, mask))
            total, fixed = call(
                functools.partial(join_kernel, axis, mask, groups, reverse),
                [shape(total.shape)] * 2,
                [VMEM] * 2,
                20 * big,
            )(total, other)
            parts.append(fixed)
        axis, mask = levels[-1]
        return parts, lax.ppermute(total[width:], axis, xor_pairs(axis, mask))

    parts, top = scan_levels(total, False)

    bmap, bstrand, bpick = call(
        functools.partial(backward_kernel, groups, share, span, owned),
        [shape((width, width)), shape((STRANDS, width, width)),
         shape((share, width, width), BF16)],
        [SMEM] + [VMEM] * groups,
        400 * big,
    )(regime, *smooth)

    filtered, pushed, zero, total = call(
        lambda *refs: filter_kernel(levels, groups, share, span, owned, *refs[:-5],
                                    refs[-4], refs[-3], refs[-2], refs[-5], refs[-1]),
        [shape((span, rows, width))] * 2
        + [shape((STRANDS, rows, width)), shape((width + rows, width))],
        [SMEM] + [VMEM] * (len(levels) - 1 + 5 + groups + 1),
        100 * big,
    )(regime, *parts, top, fstrand, bstrand, fpick, bpick, *meas, bmap)

    parts, top = scan_levels(total, True)

    outs = call(
        functools.partial(smooth_kernel, levels, groups, share, span),
        [shape((span, tracks, width))] * groups,
        [VMEM] * (len(levels) - 1 + 6),
        50 * big,
    )(*parts, top, bstrand, bpick, filtered, pushed, zero)

    outs = exchange(outs)
    return call(
        functools.partial(collect_kernel, groups, span),
        [shape((length, tracks, width))],
        [VMEM] * groups,
        big,
    )(*outs)[0]


def solution(mesh):
    placed = (
        P("tm", "track", None),
        P("track", None, None),
        P("track", None, None),
        P("track", None),
        P("tm"),
    )
    return jax.shard_map(
        body, mesh=mesh, in_specs=placed, out_specs=P("tm", "track", None), check_vma=False
    )
```

```python
import functools

import jax
import jax.numpy as jnp
from jax import lax
from jax.experimental import pallas as pl
from jax.experimental.pallas import tpu as pltpu
from jax.sharding import PartitionSpec as P


F32 = jnp.float32
BF16 = jnp.bfloat16
VMEM = pl.BlockSpec(memory_space=pltpu.VMEM)
SMEM = pl.BlockSpec(memory_space=pltpu.SMEM)
HBM = pl.BlockSpec(memory_space=pltpu.HBM)
STRANDS = 4
GRANT = 16 * 1024 * 1024


def xor_pairs(axis, mask):
    count = lax.axis_size(axis)
    return [(source, source ^ mask) for source in range(count)]


def call(kernel, outs, ins, cost, scratch=()):
    return pl.pallas_call(
        kernel,
        out_shape=outs,
        in_specs=ins,
        out_specs=[VMEM] * len(outs),
        scratch_shapes=list(scratch),
        compiler_params=pltpu.CompilerParams(vmem_limit_bytes=GRANT),
        cost_estimate=pl.CostEstimate(flops=cost, bytes_accessed=cost // 64, transcendentals=0),
    )


def shape(dims, dtype=F32):
    return jax.ShapeDtypeStruct(dims, dtype)


def split(value):
    high = value.astype(BF16)
    low = (value - high.astype(F32)).astype(BF16)
    return high, low


def times_rows(value, doubled):
    pieces = jnp.concatenate(split(value), axis=1)
    return lax.dot_general(
        pieces, doubled, (((1,), (1,)), ((), ())), preferred_element_type=F32
    )


def times(value, matrix):
    high, low = split(value)
    upper, lower = split(matrix)
    left = jnp.concatenate([high, low, high], axis=1)
    right = jnp.concatenate([upper, upper, lower], axis=0)
    return jnp.dot(left, right, preferred_element_type=F32)


def compose(earlier, later, width):
    product = times(earlier, later[:width])
    return jnp.concatenate([product[:width], product[width:] + later[width:]], axis=0)


def place_of():
    return lax.axis_index("track")


def choose(index, options):
    value = options[0]
    for j in range(1, len(options)):
        value = jnp.where(index == j, options[j], value)
    return value


def measured_kernel(groups, share, span, regime_ref, gains_ref, obs_ref, *refs):
    outs, table = (refs[:groups], refs[groups])
    me = place_of()
    owned = gains_ref.shape[0]
    table[...] = gains_ref[...].astype(F32)
    tracks, width = obs_ref.shape[1:]
    for j in range(groups):
        peer = me ^ j
        first = pl.multiple_of(peer * span, span)
        outs[j][0:span] = obs_ref[pl.ds(first, span)]
        for b in range(share):
            at = jnp.clip(regime_ref[peer * share + b] - me * owned, 0, owned - 1)
            outs[j][span + b] = jnp.broadcast_to(table[pl.ds(at, 1), :], (tracks, width))


def gather_kernel(groups, share, regime_ref, table_ref, *refs):
    outs, sems = (refs[:groups], refs[groups])
    me = place_of()
    owned = table_ref.shape[0]
    for j in range(groups):
        peer = me ^ j
        for b in range(share):
            at = jnp.clip(regime_ref[peer * share + b] - me * owned, 0, owned - 1)
            pltpu.make_async_copy(table_ref.at[at], outs[j].at[b], sems.at[j]).start()
    for j in range(groups):
        pltpu.make_async_copy(table_ref.at[pl.ds(0, share)], outs[j], sems.at[j]).wait()


def pick_matrix(regime_ref, share, owned, me, parts, b):
    source = (regime_ref[me * share + b] // owned) ^ me
    return choose(source, [part[b] for part in parts])


def doubled(matrix):
    return jnp.concatenate([matrix, matrix], axis=1)


def gain_rows(regime_ref, share, owned, me, span, parts, b):
    source = (regime_ref[me * share + b] // owned) ^ me
    return choose(source, [part[span + b][0:1] for part in parts])


def step_rows(parts, t):
    return jnp.concatenate([part[t] for part in parts], axis=0)


def forward_kernel(groups, share, span, owned, regime_ref, *refs):
    mats, meas = (refs[:groups], refs[groups : 2 * groups])
    total_ref, strand_ref, picked_ref = refs[2 * groups :]
    me = place_of()
    width = mats[0].shape[1]
    rows = groups * meas[0].shape[1]
    dwell = span // share
    per = share // STRANDS
    weights, gains = ([], [])
    for b in range(share):
        picked = pick_matrix(regime_ref, share, owned, me, mats, b)
        picked_ref[b] = picked
        weights.append(doubled(picked))
        gains.append(gain_rows(regime_ref, share, owned, me, span, meas, b))
    unit = (
        lax.broadcasted_iota(jnp.int32, (width, width), 0)
        == lax.broadcasted_iota(jnp.int32, (width, width), 1)
    ).astype(F32)
    start = jnp.concatenate([unit, jnp.zeros((rows, width), F32)], axis=0)
    states = [start] * STRANDS
    for i in range(per * dwell):
        for s in range(STRANDS):
            b = s * per + i // dwell
            t = b * dwell + i % dwell
            moved = times_rows(states[s], weights[b])
            kept = moved * (1.0 - gains[b])
            driven = gains[b] * step_rows(meas, t)
            states[s] = jnp.concatenate([kept[:width], kept[width:] + driven], axis=0)
    for s in range(STRANDS):
        strand_ref[s] = states[s]
    while len(states) > 1:
        states = [compose(states[i], states[i + 1], width) for i in range(0, len(states), 2)]
    total_ref[...] = states[0]


def backward_kernel(groups, share, span, owned, regime_ref, *refs):
    mats = refs[:groups]
    total_ref, strand_ref, picked_ref = refs[groups:]
    me = place_of()
    width = mats[0].shape[1]
    dwell = span // share
    per = share // STRANDS
    weights = []
    for b in range(share):
        picked = pick_matrix(regime_ref, share, owned, me, mats, b)
        picked_ref[b] = picked
        weights.append(doubled(picked))
    unit = (
        lax.broadcasted_iota(jnp.int32, (width, width), 0)
        == lax.broadcasted_iota(jnp.int32, (width, width), 1)
    ).astype(F32)
    states = [unit] * STRANDS
    for i in range(per * dwell):
        for s in range(STRANDS):
            b = s * per + per - 1 - i // dwell
            states[s] = times_rows(states[s], weights[b])
    for s in range(STRANDS):
        strand_ref[s] = states[s]
    while len(states) > 1:
        states = [times(states[i + 1], states[i]) for i in range(0, len(states), 2)]
    total_ref[...] = states[0]


def swapped(rows, mask, groups):
    block = rows.shape[0] // groups
    return jnp.concatenate(
        [rows[(j ^ mask) * block : ((j ^ mask) + 1) * block] for j in range(groups)], axis=0
    )


def is_later(axis, mask):
    return (lax.axis_index(axis) & mask) != 0


def join_kernel(axis, mask, groups, reverse, own_ref, other_ref, joined_ref, fixed_ref):
    width = own_ref.shape[1]
    own, other = (own_ref[...], other_ref[...])
    if axis == "track":
        other = jnp.concatenate([other[:width], swapped(other[width:], mask, groups)], axis=0)
    fixed_ref[...] = other
    swap = is_later(axis, mask)
    if reverse:
        swap = jnp.logical_not(swap)
    joined_ref[...] = compose(jnp.where(swap, other, own), jnp.where(swap, own, other), width)


def carried(levels, parts, top, reverse):
    width = parts[0].shape[1]
    axis, mask = levels[-1]
    goes = is_later(axis, mask)
    if reverse:
        goes = jnp.logical_not(goes)
    carry = jnp.where(goes, top, jnp.zeros_like(top))
    for (axis, mask), part in zip(levels[-2::-1], parts[::-1]):
        goes = is_later(axis, mask)
        if reverse:
            goes = jnp.logical_not(goes)
        carry = jnp.where(goes, times(carry, part[:width]) + part[width:], carry)
    return carry


def filter_kernel(levels, groups, share, span, owned, regime_ref, *refs):
    count = len(levels) - 1
    parts = refs[:count]
    top_ref, fstrand_ref, bstrand_ref, fpick_ref, bpick_ref = refs[count : count + 5]
    meas = refs[count + 5 : count + 5 + groups]
    filtered_ref, pushed_ref, out_ref, bmap_ref, total_ref = refs[count + 5 + groups :]
    me = place_of()
    width = fpick_ref.shape[1]
    rows = top_ref.shape[0]
    dwell = span // share
    per = share // STRANDS
    carry = carried(levels, [part[...] for part in parts], top_ref[...], False)
    starts = [carry]
    for s in range(STRANDS - 1):
        strand = fstrand_ref[s]
        starts.append(times(starts[-1], strand[:width]) + strand[width:])
    gains = [gain_rows(regime_ref, share, owned, me, span, meas, b) for b in range(share)]
    weights = [doubled(fpick_ref[b]) for b in range(share)]
    states = starts
    pushes = [None] * span
    for i in range(per * dwell):
        for s in range(STRANDS):
            b = s * per + i // dwell
            t = b * dwell + i % dwell
            ahead = times_rows(states[s], weights[b])
            pushes[t] = gains[b] * (step_rows(meas, t) - ahead)
            states[s] = ahead + pushes[t]
            filtered_ref[t] = states[s]
            pushed_ref[t] = pushes[t]
    weights = [doubled(bpick_ref[b]) for b in range(share)]
    states = [None] * STRANDS
    for i in range(per * dwell):
        for s in range(STRANDS):
            b = s * per + per - 1 - i // dwell
            t = b * dwell + dwell - 1 - i % dwell
            state = pushes[t] if i == 0 else states[s] + pushes[t]
            states[s] = times_rows(state, weights[b])
    state = states[-1]
    for s in range(STRANDS - 2, -1, -1):
        state = times(state, bstrand_ref[s]) + states[s]
    for s in range(STRANDS):
        out_ref[s] = states[s]
    total_ref[0:width] = bmap_ref[...]
    total_ref[width:] = state


def smooth_kernel(levels, groups, share, span, *refs):
    count = len(levels) - 1
    parts = refs[:count]
    top_ref, bstrand_ref, bpick_ref, filtered_ref, pushed_ref, zero_ref = refs[count : count + 6]
    outs = refs[count + 6 :]
    dwell = span // share
    per = share // STRANDS
    tracks = outs[0].shape[1]
    carry = carried(levels, [part[...] for part in parts], top_ref[...], True)
    starts = [carry]
    for s in range(STRANDS - 1, 0, -1):
        starts.append(times(starts[-1], bstrand_ref[s]) + zero_ref[s])
    states = starts[::-1]
    weights = [doubled(bpick_ref[b]) for b in range(share)]
    for i in range(per * dwell):
        for s in range(STRANDS):
            b = s * per + per - 1 - i // dwell
            t = b * dwell + dwell - 1 - i % dwell
            value = filtered_ref[t] + states[s]
            for j in range(groups):
                outs[j][t] = value[j * tracks : (j + 1) * tracks]
            if i < per * dwell - 1:
                states[s] = times_rows(states[s] + pushed_ref[t], weights[b])


def collect_kernel(groups, span, *refs):
    parts, out_ref = (refs[:groups], refs[groups])
    me = place_of()
    for j in range(groups):
        first = pl.multiple_of((me ^ j) * span, span)
        out_ref[pl.ds(first, span)] = parts[j][...]


def body(observations, dynamics, smoother_gain, gains, regime):
    length, tracks, width = observations.shape
    blocks = regime.shape[0]
    groups = lax.axis_size("track")
    dwell = length // blocks
    share = blocks // groups
    span = share * dwell
    owned = dynamics.shape[0]
    rows = groups * tracks
    levels = []
    for axis in ("track", "tm"):
        mask = 1
        while mask < lax.axis_size(axis):
            levels.append((axis, mask))
            mask *= 2
    big = width * width * width

    def exchange(values):
        return [values[0]] + [
            lax.ppermute(values[j], "track", xor_pairs("track", j)) for j in range(1, groups)
        ]

    meas = call(
        functools.partial(measured_kernel, groups, share, span),
        [shape((span + share, tracks, width))] * groups,
        [SMEM, VMEM, VMEM],
        big,
        [pltpu.VMEM((owned, width), F32)],
    )(regime, gains, observations)
    meas = exchange(meas)

    def gathered(table):
        return call(
            functools.partial(gather_kernel, groups, share),
            [shape((share, width, width), BF16)] * groups,
            [SMEM, HBM],
            4 * big,
            [pltpu.SemaphoreType.DMA((groups,))],
        )(regime, table)

    trans = exchange(gathered(dynamics))
    smooth = exchange(gathered(smoother_gain))

    total, fstrand, fpick = call(
        functools.partial(forward_kernel, groups, share, span, owned),
        [shape((width + rows, width)), shape((STRANDS, width + rows, width)),
         shape((share, width, width), BF16)],
        [SMEM] + [VMEM] * (2 * groups),
        400 * big,
    )(regime, *trans, *meas)

    def scan_levels(total, reverse):
        parts = []
        for axis, mask in levels[:-1]:
            other = lax.ppermute(total, axis, xor_pairs(axis, mask))
            total, fixed = call(
                functools.partial(join_kernel, axis, mask, groups, reverse),
                [shape(total.shape)] * 2,
                [VMEM] * 2,
                20 * big,
            )(total, other)
            parts.append(fixed)
        axis, mask = levels[-1]
        return parts, lax.ppermute(total[width:], axis, xor_pairs(axis, mask))

    parts, top = scan_levels(total, False)

    bmap, bstrand, bpick = call(
        functools.partial(backward_kernel, groups, share, span, owned),
        [shape((width, width)), shape((STRANDS, width, width)),
         shape((share, width, width), BF16)],
        [SMEM] + [VMEM] * groups,
        400 * big,
    )(regime, *smooth)

    filtered, pushed, zero, total = call(
        lambda *refs: filter_kernel(levels, groups, share, span, owned, *refs[:-5],
                                    refs[-4], refs[-3], refs[-2], refs[-5], refs[-1]),
        [shape((span, rows, width))] * 2
        + [shape((STRANDS, rows, width)), shape((width + rows, width))],
        [SMEM] + [VMEM] * (len(levels) - 1 + 5 + groups + 1),
        100 * big,
    )(regime, *parts, top, fstrand, bstrand, fpick, bpick, *meas, bmap)

    parts, top = scan_levels(total, True)

    outs = call(
        functools.partial(smooth_kernel, levels, groups, share, span),
        [shape((span, tracks, width))] * groups,
        [VMEM] * (len(levels) - 1 + 6),
        50 * big,
    )(*parts, top, bstrand, bpick, filtered, pushed, zero)

    outs = exchange(outs)
    return call(
        functools.partial(collect_kernel, groups, span),
        [shape((length, tracks, width))],
        [VMEM] * groups,
        big,
    )(*outs)[0]


def solution(mesh):
    placed = (
        P("tm", "track", None),
        P("track", None, None),
        P("track", None, None),
        P("track", None),
        P("tm"),
    )
    return jax.shard_map(
        body, mesh=mesh, in_specs=placed, out_specs=P("tm", "track", None), check_vma=False
    )
```

```python
import functools

import jax
import jax.numpy as jnp
from jax import lax
from jax.experimental import pallas as pl
from jax.experimental.pallas import tpu as pltpu
from jax.sharding import PartitionSpec as P


F32 = jnp.float32
BF16 = jnp.bfloat16
VMEM = pl.BlockSpec(memory_space=pltpu.VMEM)
SMEM = pl.BlockSpec(memory_space=pltpu.SMEM)
HBM = pl.BlockSpec(memory_space=pltpu.HBM)
STRANDS = 4
GRANT = 16 * 1024 * 1024


def call(kernel, outs, ins, cost, scratch=()):
    return pl.pallas_call(
        kernel,
        out_shape=outs,
        in_specs=ins,
        out_specs=[VMEM] * len(outs),
        scratch_shapes=list(scratch),
        compiler_params=pltpu.CompilerParams(vmem_limit_bytes=GRANT),
        cost_estimate=pl.CostEstimate(flops=cost, bytes_accessed=cost // 64, transcendentals=0),
    )


def shape(dims, dtype=F32):
    return jax.ShapeDtypeStruct(dims, dtype)


def split(value):
    high = value.astype(BF16)
    low = (value - high.astype(F32)).astype(BF16)
    return high, low


def times_rows(value, doubled):
    pieces = jnp.concatenate(split(value), axis=1)
    return lax.dot_general(
        pieces, doubled, (((1,), (1,)), ((), ())), preferred_element_type=F32
    )


def times(value, matrix):
    high, low = split(value)
    upper, lower = split(matrix)
    left = jnp.concatenate([high, low, high], axis=1)
    right = jnp.concatenate([upper, upper, lower], axis=0)
    return jnp.dot(left, right, preferred_element_type=F32)


def compose(first, second):
    width = first.shape[1]
    product = times(first, second[:width])
    return jnp.concatenate([product[:width], product[width:] + second[width:]], axis=0)


def apply(state, chart):
    width = chart.shape[1]
    return times(state, chart[:width]) + chart[width:]


def unit_chart(width, rows):
    unit = (
        lax.broadcasted_iota(jnp.int32, (width, width), 0)
        == lax.broadcasted_iota(jnp.int32, (width, width), 1)
    ).astype(F32)
    return jnp.concatenate([unit, jnp.zeros((rows, width), F32)], axis=0)


def choose(index, options):
    value = options[0]
    for j in range(1, len(options)):
        value = jnp.where(index == j, options[j], value)
    return value


def swapped(rows, mask, groups):
    block = rows.shape[0] // groups
    return jnp.concatenate(
        [rows[(j ^ mask) * block : ((j ^ mask) + 1) * block] for j in range(groups)], axis=0
    )


def doubled(matrix):
    return jnp.concatenate([matrix, matrix], axis=1)


def step_rows(parts, t):
    return jnp.concatenate([part[t] for part in parts], axis=0)


class Plan:
    def __init__(self, groups, share, dwell, owned, tracks, width):
        self.groups, self.share, self.dwell = groups, share, dwell
        self.owned, self.tracks, self.width = owned, tracks, width
        self.span, self.rows = share * dwell, groups * tracks
        self.extra = -(-share // tracks)
        self.per = share // STRANDS
        self.length = self.per * dwell

    def here(self, regime_ref, peer, b):
        local = regime_ref[peer * self.share + b] - lax.axis_index("track") * self.owned
        return jnp.clip(local, 0, self.owned - 1)

    def source(self, regime_ref, b):
        me = lax.axis_index("track")
        return (regime_ref[me * self.share + b] // self.owned) ^ me

    def gain_row(self, regime_ref, meas, b):
        step, row = self.span + b // self.tracks, b % self.tracks
        return choose(
            self.source(regime_ref, b), [part[step][row : row + 1] for part in meas]
        )

    def forward_steps(self):
        for i in range(self.length):
            for s in range(STRANDS):
                b = s * self.per + i // self.dwell
                yield i, s, b, b * self.dwell + i % self.dwell

    def backward_steps(self):
        for i in range(self.length):
            for s in range(STRANDS):
                b = s * self.per + self.per - 1 - i // self.dwell
                yield i, s, b, b * self.dwell + self.dwell - 1 - i % self.dwell


def gather_rows(plan, regime_ref, table_ref, outs, sems):
    for j in range(plan.groups):
        peer = lax.axis_index("track") ^ j
        for b in range(plan.share):
            at = plan.here(regime_ref, peer, b)
            pltpu.make_async_copy(table_ref.at[at], outs[j].at[b], sems.at[j]).start()


def gather_wait(plan, table_ref, outs, sems):
    for j in range(plan.groups):
        rows = table_ref.at[pl.ds(0, plan.share)]
        pltpu.make_async_copy(rows, outs[j], sems.at[j]).wait()


def gather_kernel(plan, regime_ref, table_ref, *refs):
    outs, sems = (refs[: plan.groups], refs[plan.groups])
    gather_rows(plan, regime_ref, table_ref, outs, sems)
    gather_wait(plan, table_ref, outs, sems)


def second_gather_kernel(plan, regime_ref, table_ref, gains_ref, obs_ref, *refs):
    groups, tracks = (plan.groups, plan.tracks)
    mats, meas = (refs[:groups], refs[groups : 2 * groups])
    gain_ref, sems = refs[2 * groups :]
    gather_rows(plan, regime_ref, table_ref, mats, sems)
    gain_ref[...] = gains_ref[...].astype(F32)
    for j in range(groups):
        peer = lax.axis_index("track") ^ j
        first = pl.multiple_of(peer * plan.span, plan.span)
        meas[j][0 : plan.span] = obs_ref[pl.ds(first, plan.span)]
        for e in range(plan.extra):
            blocks = [min(e * tracks + i, plan.share - 1) for i in range(tracks)]
            meas[j][plan.span + e] = jnp.concatenate(
                [gain_ref[pl.ds(plan.here(regime_ref, peer, b), 1), :] for b in blocks], axis=0
            )
    gather_wait(plan, table_ref, mats, sems)


def picked_weights(plan, regime_ref, mats, picked_ref):
    weights = []
    for b in range(plan.share):
        picked = choose(plan.source(regime_ref, b), [part[b] for part in mats])
        picked_ref[b] = picked
        weights.append(doubled(picked))
    return weights


def forward_kernel(plan, regime_ref, *refs):
    groups, width = (plan.groups, plan.width)
    mats, meas = (refs[:groups], refs[groups : 2 * groups])
    total_ref, strand_ref, picked_ref = refs[2 * groups :]
    weights = picked_weights(plan, regime_ref, mats, picked_ref)
    gains = [plan.gain_row(regime_ref, meas, b) for b in range(plan.share)]
    states = [unit_chart(width, plan.rows)] * STRANDS
    for i, s, b, t in plan.forward_steps():
        kept = times_rows(states[s], weights[b]) * (1.0 - gains[b])
        driven = gains[b] * step_rows(meas, t)
        states[s] = jnp.concatenate([kept[:width], kept[width:] + driven], axis=0)
    for s in range(STRANDS):
        strand_ref[s] = states[s]
    while len(states) > 1:
        states = [compose(states[i], states[i + 1]) for i in range(0, len(states), 2)]
    total_ref[...] = states[0]


def backward_kernel(plan, regime_ref, *refs):
    groups, width = (plan.groups, plan.width)
    mats, pushed_ref = (refs[:groups], refs[groups])
    total_ref, strand_ref, picked_ref = refs[groups + 1 :]
    weights = picked_weights(plan, regime_ref, mats, picked_ref)
    states = [unit_chart(width, plan.rows)] * STRANDS
    for i, s, b, t in plan.backward_steps():
        state = states[s]
        state = jnp.concatenate([state[:width], state[width:] + pushed_ref[t]], axis=0)
        states[s] = times_rows(state, weights[b])
    for s in range(STRANDS):
        strand_ref[s] = states[s]
    while len(states) > 1:
        states = [compose(states[i + 1], states[i]) for i in range(0, len(states), 2)]
    total_ref[...] = states[0]


def group_kernel(plan, reverse, *refs):
    groups, width = (plan.groups, plan.width)
    parts, (total_ref, before_ref) = (refs[:groups], refs[groups:])
    fixed = []
    for j in range(groups):
        part = parts[j][...]
        fixed.append(jnp.concatenate([part[:width], swapped(part[width:], j, groups)], axis=0))
    me = lax.axis_index("track")
    order = list(range(groups))[::-1] if reverse else list(range(groups))
    charts = [choose(me ^ q, fixed) for q in order]
    place = groups - 1 - me if reverse else me
    befores = [unit_chart(width, plan.rows), charts[0]]
    while len(befores) < groups:
        befores.append(compose(befores[-1], charts[len(befores) - 1]))
    before_ref[...] = choose(place, befores)
    while len(charts) > 1:
        odd = charts[len(charts) // 2 * 2 :]
        charts = [compose(charts[i], charts[i + 1]) for i in range(0, len(charts) - 1, 2)] + odd
    total_ref[...] = charts[0]


def is_second(mask, reverse):
    second = (lax.axis_index("tm") & mask) != 0
    return jnp.logical_not(second) if reverse else second


def pair_kernel(mask, reverse, last, own_ref, other_ref, before_ref, joined_ref, after_ref):
    width = own_ref.shape[1]
    own, other, before = (own_ref[...], other_ref[...], before_ref[...])
    second = is_second(mask, reverse)
    earlier, later = (jnp.where(second, other, own), jnp.where(second, own, other))
    if last:
        joined_ref[...] = apply(earlier[width:], later)
    else:
        joined_ref[...] = compose(earlier, later)
    after_ref[...] = jnp.where(second, compose(other, before), before)


def entering(far_ref, before_ref, reverse):
    far = far_ref[...]
    return apply(jnp.where(is_second(lax.axis_size("tm") // 2, reverse), far, jnp.zeros_like(far)), before_ref[...])


def filter_kernel(plan, regime_ref, before_ref, far_ref, strand_ref, picked_ref, *refs):
    meas, (filtered_ref, pushed_ref) = (refs[: plan.groups], refs[plan.groups :])
    states = [entering(far_ref, before_ref, False)]
    for s in range(STRANDS - 1):
        states.append(apply(states[-1], strand_ref[s]))
    gains = [plan.gain_row(regime_ref, meas, b) for b in range(plan.share)]
    weights = [doubled(picked_ref[b]) for b in range(plan.share)]
    for i, s, b, t in plan.forward_steps():
        ahead = times_rows(states[s], weights[b])
        pushed = gains[b] * (step_rows(meas, t) - ahead)
        states[s] = ahead + pushed
        filtered_ref[t] = states[s]
        pushed_ref[t] = pushed


def smooth_kernel(
    plan, before_ref, far_ref, strand_ref, picked_ref, filtered_ref, pushed_ref, *outs
):
    tracks = plan.tracks
    states = [entering(far_ref, before_ref, True)]
    for s in range(STRANDS - 1, 0, -1):
        states.append(apply(states[-1], strand_ref[s]))
    states = states[::-1]
    weights = [doubled(picked_ref[b]) for b in range(plan.share)]
    for i, s, b, t in plan.backward_steps():
        value = filtered_ref[t] + states[s]
        for j in range(plan.groups):
            outs[j][t] = value[j * tracks : (j + 1) * tracks]
        if i < plan.length - 1:
            states[s] = times_rows(states[s] + pushed_ref[t], weights[b])


def collect_kernel(plan, *refs):
    parts, out_ref = (refs[: plan.groups], refs[plan.groups])
    for j in range(plan.groups):
        first = pl.multiple_of((lax.axis_index("track") ^ j) * plan.span, plan.span)
        out_ref[pl.ds(first, plan.span)] = parts[j][...]


def body(observations, dynamics, smoother_gain, gains, regime):
    length, tracks, width = observations.shape
    blocks = regime.shape[0]
    groups, spans = (lax.axis_size("track"), lax.axis_size("tm"))
    owned = dynamics.shape[0]
    plan = Plan(groups, blocks // groups, length // blocks, owned, tracks, width)
    chart = shape((width + plan.rows, width))
    offset = shape((plan.rows, width))
    strands = shape((STRANDS,) + chart.shape)
    mats = [shape((plan.share, width, width), BF16)] * groups
    unit = width * width * width
    regime, observations, dynamics, smoother_gain, gains = [
        pltpu.with_memory_space_constraint(value, pltpu.HBM)
        for value in (regime, observations, dynamics, smoother_gain, gains)
    ]

    def swap(value, mask, axis):
        pairs = [(source, source ^ mask) for source in range(lax.axis_size(axis))]
        return lax.ppermute(value, axis, pairs)

    def exchange(values):
        return [values[0]] + [swap(values[j], j, "track") for j in range(1, groups)]

    sems = pltpu.SemaphoreType.DMA((groups,))
    trans = call(
        functools.partial(gather_kernel, plan), mats, [SMEM, HBM], unit, [sems]
    )(regime, dynamics)
    trans = exchange(trans)
    gathered = call(
        functools.partial(second_gather_kernel, plan),
        mats + [shape((plan.span + plan.extra, tracks, width))] * groups,
        [SMEM, HBM, VMEM, VMEM],
        unit,
        [pltpu.VMEM((owned, width), F32), sems],
    )(regime, smoother_gain, gains, observations)
    meas = exchange(gathered[groups:])

    total, fstrand, fpick = call(
        functools.partial(forward_kernel, plan),
        [chart, strands, shape((plan.share, width, width), BF16)],
        [SMEM] + [VMEM] * (2 * groups),
        400 * unit,
    )(regime, *trans, *meas)

    smooth, total = lax.optimization_barrier((gathered[:groups], total))

    def spread(total):
        return exchange([total] * groups)

    def across(total, reverse):
        total, before = call(
            functools.partial(group_kernel, plan, reverse),
            [chart, chart],
            [VMEM] * groups,
            20 * unit,
        )(*spread(total))
        stride = 1
        while 2 * stride < spans:
            last = 4 * stride >= spans
            total, before = call(
                functools.partial(pair_kernel, stride, reverse, last),
                [offset if last else chart, chart],
                [VMEM] * 3,
                20 * unit,
            )(total, swap(total, stride, "tm"), before)
            stride *= 2
        total = total[-plan.rows :] if stride == 1 else total
        return before, swap(total, stride, "tm")

    entry = across(total, False)
    filtered, pushed = call(
        functools.partial(filter_kernel, plan),
        [shape((plan.span, plan.rows, width))] * 2,
        [SMEM] + [VMEM] * (4 + groups),
        100 * unit,
    )(regime, *entry, fstrand, fpick, *meas)

    smooth = exchange(smooth)
    total, bstrand, bpick = call(
        functools.partial(backward_kernel, plan),
        [chart, strands, shape((plan.share, width, width), BF16)],
        [SMEM] + [VMEM] * (groups + 1),
        400 * unit,
    )(regime, *smooth, pushed)

    entry = across(total, True)
    outs = call(
        functools.partial(smooth_kernel, plan),
        [shape((plan.span, tracks, width))] * groups,
        [VMEM] * 6,
        50 * unit,
    )(*entry, bstrand, bpick, filtered, pushed)
    return call(
        functools.partial(collect_kernel, plan),
        [shape((length, tracks, width))],
        [VMEM] * groups,
        unit,
    )(*exchange(outs))[0]


def solution(mesh):
    placed = (
        P("tm", "track", None),
        P("track", None, None),
        P("track", None, None),
        P("track", None),
        P("tm"),
    )

    return jax.shard_map(
        body, mesh=mesh, in_specs=placed, out_specs=P("tm", "track", None), check_vma=False
    )
```

```python
import functools

import jax
import jax.numpy as jnp
from jax import lax
from jax.experimental import pallas as pl
from jax.experimental.pallas import tpu as pltpu
from jax.sharding import PartitionSpec as P


F32 = jnp.float32
BF16 = jnp.bfloat16
VMEM = pl.BlockSpec(memory_space=pltpu.VMEM)
SMEM = pl.BlockSpec(memory_space=pltpu.SMEM)
HBM = pl.BlockSpec(memory_space=pltpu.HBM)
GRANT = 16 * 1024 * 1024


def call(kernel, outs, ins, cost, scratch=()):
    return pl.pallas_call(
        kernel,
        out_shape=outs,
        in_specs=ins,
        out_specs=[VMEM] * len(outs),
        scratch_shapes=list(scratch),
        compiler_params=pltpu.CompilerParams(vmem_limit_bytes=GRANT),
        cost_estimate=pl.CostEstimate(flops=cost, bytes_accessed=cost // 64, transcendentals=0),
    )


def shape(dims, dtype=F32):
    return jax.ShapeDtypeStruct(dims, dtype)


def split(value):
    high = value.astype(BF16)
    low = (value - high.astype(F32)).astype(BF16)
    return high, low


def times_rows(value, doubled):
    pieces = jnp.concatenate(split(value), axis=1)
    return lax.dot_general(
        pieces, doubled, (((1,), (1,)), ((), ())), preferred_element_type=F32
    )


def times(value, matrix):
    high, low = split(value)
    upper, lower = split(matrix)
    left = jnp.concatenate([high, low, high], axis=1)
    right = jnp.concatenate([upper, upper, lower], axis=0)
    return jnp.dot(left, right, preferred_element_type=F32)


def compose(first, second):
    width = first.shape[1]
    product = times(first, second[:width])
    return jnp.concatenate([product[:width], product[width:] + second[width:]], axis=0)


def apply(state, chart):
    width = chart.shape[1]
    return times(state, chart[:width]) + chart[width:]


def unit_matrix(width):
    rows = lax.broadcasted_iota(jnp.int32, (width, width), 0)
    return (rows == lax.broadcasted_iota(jnp.int32, (width, width), 1)).astype(F32)


def unit_chart(width, rows):
    return jnp.concatenate([unit_matrix(width), jnp.zeros((rows, width), F32)], axis=0)


def choose(index, options):
    value = options[0]
    for j in range(1, len(options)):
        value = jnp.where(index == j, options[j], value)
    return value


def swapped(rows, mask, groups):
    block = rows.shape[0] // groups
    return jnp.concatenate(
        [rows[(j ^ mask) * block : ((j ^ mask) + 1) * block] for j in range(groups)], axis=0
    )


def doubled(matrix):
    return jnp.concatenate([matrix, matrix], axis=1)


def step_rows(parts, t):
    return jnp.concatenate([part[t] for part in parts], axis=0)


class Plan:
    def __init__(self, groups, share, dwell, owned, tracks, width):
        self.groups, self.share, self.dwell = groups, share, dwell
        self.owned, self.tracks, self.width = owned, tracks, width
        self.span, self.rows = share * dwell, groups * tracks
        self.extra = -(-share // tracks)

    def local(self, regime_ref, peer, b):
        return regime_ref[peer * self.share + b] - lax.axis_index("track") * self.owned

    def here(self, regime_ref, peer, b):
        return jnp.clip(self.local(regime_ref, peer, b), 0, self.owned - 1)

    def source(self, regime_ref, b):
        me = lax.axis_index("track")
        return (regime_ref[me * self.share + b] // self.owned) ^ me

    def gain_row(self, regime_ref, meas, b):
        step, row = self.span + b // self.tracks, b % self.tracks
        return choose(
            self.source(regime_ref, b), [part[step][row : row + 1] for part in meas]
        )

    def forward_steps(self, first, last):
        return [(b, b * self.dwell + i) for i in range(self.dwell) for b in range(first, last)]

    def backward_steps(self, first, last):
        turn = self.dwell - 1
        return [(b, t + turn - 2 * (t % self.dwell)) for b, t in self.forward_steps(first, last)]


def piece_of(pieces, b):
    for piece in pieces:
        if b < piece.shape[0]:
            return piece.at[b]
        b -= piece.shape[0]


def each_row(plan, regime_ref, table_ref, targets, sem, act):
    for j, pieces in targets:
        peer = lax.axis_index("track") ^ j
        for b in range(plan.share):
            at = plan.local(regime_ref, peer, b)

            @pl.when(jnp.logical_and(at >= 0, at < plan.owned))
            def _():
                copy = pltpu.make_async_copy(table_ref.at[at], piece_of(pieces, b), sem)
                copy.start() if act else copy.wait()


def split_up(refs, layout):
    refs, found = (list(refs), [])
    for pieces in layout:
        found.append([refs.pop(0) for _ in pieces])
    return found


def gather_kernel(plan, layout, regime_ref, table_ref, *refs):
    outs, sem = (split_up(refs[:-1], layout), refs[-1])
    targets = [(j + 1, pieces) for j, pieces in enumerate(outs)]
    each_row(plan, regime_ref, table_ref, targets, sem, True)
    each_row(plan, regime_ref, table_ref, targets, sem, False)


def second_gather_kernel(plan, layout, regime_ref, first_ref, second_ref, *refs):
    own_ref, outs, sem = (refs[0], split_up(refs[1:-1], layout), refs[-1])
    targets = list(enumerate(outs))
    for act in (True, False):
        each_row(plan, regime_ref, first_ref, [(0, [own_ref])], sem, act)
        each_row(plan, regime_ref, second_ref, targets, sem, act)


def measured_kernel(plan, regime_ref, gains_ref, obs_ref, *refs):
    meas, gain_ref = (refs[:-1], refs[-1])
    gain_ref[...] = gains_ref[...].astype(F32)
    for j in range(plan.groups):
        peer = lax.axis_index("track") ^ j
        first = pl.multiple_of(peer * plan.span, plan.span)
        meas[j][0 : plan.span] = obs_ref[pl.ds(first, plan.span)]
        for e in range(plan.extra):
            blocks = [min(e * plan.tracks + i, plan.share - 1) for i in range(plan.tracks)]
            meas[j][plan.span + e] = jnp.concatenate(
                [gain_ref[pl.ds(plan.here(regime_ref, peer, b), 1), :] for b in blocks], axis=0
            )


def picked_weight(plan, regime_ref, mats, b):
    return choose(plan.source(regime_ref, b), [piece_of(pieces, b)[...] for pieces in mats])


def joined(charts):
    while len(charts) > 1:
        odd = charts[len(charts) // 2 * 2 :]
        charts = [compose(charts[i], charts[i + 1]) for i in range(0, len(charts) - 1, 2)] + odd
    return charts[0]


def running(charts):
    if len(charts) == 1:
        return charts
    pairs = running([compose(charts[i], charts[i + 1]) for i in range(0, len(charts) - 1, 2)])
    found = [charts[0]]
    for i in range(1, len(charts)):
        found.append(pairs[i // 2] if i % 2 else compose(pairs[i // 2 - 1], charts[i]))
    return found


def forward_kernel(plan, first, last, layout, regime_ref, *refs):
    count = sum(len(pieces) for pieces in layout)
    mats, refs = (split_up(refs[:count], layout), refs[count:])
    meas, refs = (refs[: plan.groups], refs[plan.groups :])
    earlier_ref, refs = (refs[0], refs[1:]) if first else (None, refs)
    strand_ref, picked_ref, total_ref = refs
    weights, gains, states = ({}, {}, {})
    for b in range(first, last):
        picked = choose(
            plan.source(regime_ref, b),
            [piece_of(mats[0], b)[...]]
            + [piece_of(pieces, b - first)[...] for pieces in mats[1:]],
        )
        picked_ref[b - first] = picked
        weights[b] = doubled(picked)
        gains[b] = plan.gain_row(regime_ref, meas, b)
        states[b] = unit_chart(plan.width, plan.rows)
    for b, t in plan.forward_steps(first, last):
        kept = times_rows(states[b], weights[b]) * (1.0 - gains[b])
        driven = gains[b] * step_rows(meas, t)
        states[b] = jnp.concatenate(
            [kept[: plan.width], kept[plan.width :] + driven], axis=0
        )
    for b in range(first, last):
        strand_ref[b - first] = states[b]
    total = joined(list(states.values()))
    total_ref[...] = compose(earlier_ref[...], total) if first else total


def gain_levels(charts):
    found = [charts]
    while len(charts) > 1:
        charts = [times(charts[i], charts[i + 1]) for i in range(0, len(charts), 2)]
        found.append(charts)
    return found


def backward_kernel(plan, layout, regime_ref, *refs):
    mats, (level_ref, picked_ref) = (split_up(refs[:-2], layout), refs[-2:])
    weights = []
    for b in range(plan.share):
        picked = picked_weight(plan, regime_ref, mats, b)
        picked_ref[b] = picked
        weights.append(doubled(picked))
    states = [unit_matrix(plan.width)] * plan.share
    for b, t in plan.backward_steps(0, plan.share):
        states[b] = times_rows(states[b], weights[b])
    at = 0
    for level in gain_levels(states[::-1]):
        for chart in level:
            level_ref[at] = chart
            at += 1


def forward_running_kernel(first_ref, second_ref, running_ref):
    charts = [first_ref[s] for s in range(first_ref.shape[0])]
    charts += [second_ref[s] for s in range(second_ref.shape[0] - 1)]
    for s, chart in enumerate(running(charts)):
        running_ref[s] = chart


def backward_running_kernel(level_ref, offset_ref, running_ref):
    charts = [
        jnp.concatenate([level_ref[s], offset_ref[s]], axis=0)
        for s in range(offset_ref.shape[0] - 1)
    ]
    for s, chart in enumerate(running(charts)):
        running_ref[s] = chart


def group_kernel(plan, reverse, *refs):
    groups, width = (plan.groups, plan.width)
    parts, (total_ref, before_ref) = (refs[:groups], refs[groups:])
    fixed = []
    for j in range(groups):
        part = parts[j][...]
        fixed.append(jnp.concatenate([part[:width], swapped(part[width:], j, groups)], axis=0))
    me = lax.axis_index("track")
    order = list(range(groups))[::-1] if reverse else list(range(groups))
    charts = [choose(me ^ q, fixed) for q in order]
    place = groups - 1 - me if reverse else me
    befores = [unit_chart(width, plan.rows), charts[0]]
    while len(befores) < groups:
        befores.append(compose(befores[-1], charts[len(befores) - 1]))
    before_ref[...] = choose(place, befores)
    total_ref[...] = joined(charts)


def is_second(mask, reverse):
    second = (lax.axis_index("tm") & mask) != 0
    return jnp.logical_not(second) if reverse else second


def pair_kernel(mask, reverse, last, own_ref, other_ref, before_ref, joined_ref, after_ref):
    width = own_ref.shape[1]
    own, other, before = (own_ref[...], other_ref[...], before_ref[...])
    second = is_second(mask, reverse)
    earlier, later = (jnp.where(second, other, own), jnp.where(second, own, other))
    if last:
        joined_ref[...] = apply(earlier[width:], later)
    else:
        joined_ref[...] = compose(earlier, later)
    after_ref[...] = jnp.where(second, compose(other, before), before)


def entering(far_ref, before_ref, running_ref, reverse):
    far = far_ref[...]
    second = is_second(lax.axis_size("tm") // 2, reverse)
    state = apply(jnp.where(second, far, jnp.zeros_like(far)), before_ref[...])
    return [state] + [apply(state, running_ref[s]) for s in range(running_ref.shape[0])]


def filter_kernel(plan, regime_ref, before_ref, far_ref, running_ref, fpick1_ref, fpick2_ref, *refs):
    meas, refs = (refs[: plan.groups], refs[plan.groups :])
    level_ref, bpick_ref, filtered_ref, pushed_ref, offset_ref, total_ref = refs
    states = entering(far_ref, before_ref, running_ref, False)
    gains = [plan.gain_row(regime_ref, meas, b) for b in range(plan.share)]
    weights = [
        doubled(piece_of([fpick1_ref, fpick2_ref], b)[...]) for b in range(plan.share)
    ]
    pushes = {}
    for b, t in plan.forward_steps(0, plan.share):
        ahead = times_rows(states[b], weights[b])
        pushes[t] = gains[b] * (step_rows(meas, t) - ahead)
        states[b] = ahead + pushes[t]
        filtered_ref[t] = states[b]
        pushed_ref[t] = pushes[t]
    weights = [doubled(bpick_ref[b]) for b in range(plan.share)]
    states = [None] * plan.share
    for b, t in plan.backward_steps(0, plan.share):
        state = pushes[t] if states[b] is None else states[b] + pushes[t]
        states[b] = times_rows(state, weights[b])
    states = states[::-1]
    for b in range(plan.share):
        offset_ref[b] = states[b]
    at = 0
    while len(states) > 1:
        count = len(states)
        states = [
            times(states[i], level_ref[at + i + 1]) + states[i + 1] for i in range(0, count, 2)
        ]
        at += count
    total_ref[0 : plan.width] = level_ref[at]
    total_ref[plan.width :] = states[0]


def smooth_kernel(
    plan, before_ref, far_ref, running_ref, picked_ref, filtered_ref, pushed_ref, *outs
):
    tracks = plan.tracks
    states = entering(far_ref, before_ref, running_ref, True)[::-1]
    weights = [doubled(picked_ref[b]) for b in range(plan.share)]
    for b, t in plan.backward_steps(0, plan.share):
        value = filtered_ref[t] + states[b]
        for j in range(plan.groups):
            outs[j][t] = value[j * tracks : (j + 1) * tracks]
        if t % plan.dwell > 0:
            states[b] = times_rows(states[b] + pushed_ref[t], weights[b])


def collect_kernel(plan, *refs):
    parts, out_ref = (refs[: plan.groups], refs[plan.groups])
    for j in range(plan.groups):
        first = pl.multiple_of((lax.axis_index("track") ^ j) * plan.span, plan.span)
        out_ref[pl.ds(first, plan.span)] = parts[j][...]


def body(observations, dynamics, smoother_gain, gains, regime):
    length, tracks, width = observations.shape
    blocks = regime.shape[0]
    groups, spans = (lax.axis_size("track"), lax.axis_size("tm"))
    owned = dynamics.shape[0]
    plan = Plan(groups, blocks // groups, length // blocks, owned, tracks, width)
    chart = shape((width + plan.rows, width))
    offset = shape((plan.rows, width))
    share, half = (plan.share, plan.share // 2)
    block_mats = lambda count: shape((count, width, width), BF16)
    unit = width * width * width
    regime, observations, dynamics, smoother_gain, gains = [
        pltpu.with_memory_space_constraint(value, pltpu.HBM)
        for value in (regime, observations, dynamics, smoother_gain, gains)
    ]

    def swap(value, mask, axis):
        pairs = [(source, source ^ mask) for source in range(lax.axis_size(axis))]
        return lax.ppermute(value, axis, pairs)

    def exchange(values):
        return [values[0]] + [swap(values[j], j, "track") for j in range(1, groups)]

    sem = pltpu.SemaphoreType.DMA
    halves = [[half, share - half]] * (groups - 1)
    parts = split_up(
        call(
            functools.partial(gather_kernel, plan, halves),
            [block_mats(count) for pieces in halves for count in pieces],
            [SMEM, HBM],
            unit,
            [sem],
        )(regime, dynamics),
        halves,
    )
    first = [swap(pieces[0], j + 1, "track") for j, pieces in enumerate(parts)]
    meas = call(
        functools.partial(measured_kernel, plan),
        [shape((plan.span + plan.extra, tracks, width))] * groups,
        [SMEM, VMEM, VMEM],
        unit,
        [pltpu.VMEM((owned, width), F32)],
    )(regime, gains, observations)
    meas = exchange(meas)
    second = [swap(pieces[1], j + 1, "track") for j, pieces in enumerate(parts)]
    layout = [[share]] * groups
    own, *smooth = call(
        functools.partial(second_gather_kernel, plan, layout),
        [block_mats(share)] + [block_mats(count) for pieces in layout for count in pieces],
        [SMEM, HBM, HBM],
        unit,
        [sem],
    )(regime, dynamics, smoother_gain)
    smooth = split_up(smooth, layout)
    pick = lambda begin, end, mats, more: call(
        functools.partial(forward_kernel, plan, begin, end, [[share]] + [[end - begin]] * (groups - 1)),
        [shape((end - begin,) + chart.shape), block_mats(end - begin), chart],
        [SMEM] + [VMEM] * (2 * groups + len(more)),
        200 * unit,
    )(regime, own, *mats, *meas, *more)
    fstrand1, fpick1, total = pick(0, half, first, [])
    fstrand2, fpick2, total = pick(half, share, second, [total])

    late, total = lax.optimization_barrier(([smooth[j][-1] for j in range(1, groups)], total))

    def spread(total):
        return exchange([total] * groups)

    def across(total, reverse):
        maps = spread(total)
        total, before = call(
            functools.partial(group_kernel, plan, reverse),
            [chart, chart],
            [VMEM] * groups,
            20 * unit,
        )(*maps)
        stride = 1
        while 2 * stride < spans:
            last = 4 * stride >= spans
            total, before = call(
                functools.partial(pair_kernel, stride, reverse, last),
                [offset if last else chart, chart],
                [VMEM] * 3,
                20 * unit,
            )(total, swap(total, stride, "tm"), before)
            stride *= 2
        total = total[-plan.rows :] if stride == 1 else total
        return before, swap(total, stride, "tm")

    late = [swap(value, j + 1, "track") for j, value in enumerate(late)]
    smooth = [smooth[0]] + [[value] for value in late]
    levels = 2 * share - 1
    level, bpick = call(
        functools.partial(backward_kernel, plan, layout),
        [shape((levels, width, width)), block_mats(share)],
        [SMEM] + [VMEM] * sum(len(pieces) for pieces in layout),
        300 * unit,
    )(regime, *[value for pieces in smooth for value in pieces])

    before, far = across(total, False)
    runs = [shape((share - 1,) + chart.shape)]
    (frun,) = call(forward_running_kernel, runs, [VMEM] * 2, 60 * unit)(fstrand1, fstrand2)
    filtered, pushed, offsets, total = call(
        functools.partial(filter_kernel, plan),
        [shape((plan.span, plan.rows, width))] * 2 + [shape((share,) + offset.shape), chart],
        [SMEM] + [VMEM] * (7 + groups),
        100 * unit,
    )(regime, before, far, frun, fpick1, fpick2, *meas, level, bpick)

    before, far = across(total, True)
    (brun,) = call(backward_running_kernel, runs, [VMEM] * 2, 60 * unit)(level, offsets)
    outs = call(
        functools.partial(smooth_kernel, plan),
        [shape((plan.span, tracks, width))] * groups,
        [VMEM] * 6,
        50 * unit,
    )(before, far, brun, bpick, filtered, pushed)
    return call(
        functools.partial(collect_kernel, plan),
        [shape((length, tracks, width))],
        [VMEM] * groups,
        unit,
    )(*exchange(outs))[0]


def solution(mesh):
    placed = (
        P("tm", "track", None),
        P("track", None, None),
        P("track", None, None),
        P("track", None),
        P("tm"),
    )

    return jax.shard_map(
        body, mesh=mesh, in_specs=placed, out_specs=P("tm", "track", None), check_vma=False
    )
```

```python
import functools

import jax
import jax.numpy as jnp
from jax import lax
from jax.experimental import pallas as pl
from jax.experimental.pallas import tpu as pltpu
from jax.sharding import PartitionSpec as P


F32 = jnp.float32
BF16 = jnp.bfloat16
VMEM = pl.BlockSpec(memory_space=pltpu.VMEM)
SMEM = pl.BlockSpec(memory_space=pltpu.SMEM)
HBM = pl.BlockSpec(memory_space=pltpu.HBM)
GRANT = 16 * 1024 * 1024


def call(kernel, outs, ins, cost, scratch=(), places=None):
    return pl.pallas_call(
        kernel,
        out_shape=outs,
        in_specs=ins,
        out_specs=places or [VMEM] * len(outs),
        scratch_shapes=list(scratch),
        compiler_params=pltpu.CompilerParams(vmem_limit_bytes=GRANT),
        cost_estimate=pl.CostEstimate(flops=cost, bytes_accessed=cost // 64, transcendentals=0),
    )


def shape(dims, dtype=F32):
    return jax.ShapeDtypeStruct(dims, dtype)


def split(value):
    high = value.astype(BF16)
    low = (value - high.astype(F32)).astype(BF16)
    return high, low


def times_rows(value, doubled):
    pieces = jnp.concatenate(split(value), axis=1)
    return lax.dot_general(
        pieces, doubled, (((1,), (1,)), ((), ())), preferred_element_type=F32
    )


def times(value, matrix):
    high, low = split(value)
    upper, lower = split(matrix)
    left = jnp.concatenate([high, low, high], axis=1)
    right = jnp.concatenate([upper, upper, lower], axis=0)
    return jnp.dot(left, right, preferred_element_type=F32)


def compose(first, second):
    width = first.shape[1]
    product = times(first, second[:width])
    return jnp.concatenate([product[:width], product[width:] + second[width:]], axis=0)


def apply(state, chart):
    width = chart.shape[1]
    return times(state, chart[:width]) + chart[width:]


def unit_matrix(width):
    rows = lax.broadcasted_iota(jnp.int32, (width, width), 0)
    return (rows == lax.broadcasted_iota(jnp.int32, (width, width), 1)).astype(F32)


def unit_chart(width, rows):
    return jnp.concatenate([unit_matrix(width), jnp.zeros((rows, width), F32)], axis=0)


def choose(index, options):
    value = options[0]
    for j in range(1, len(options)):
        value = jnp.where(index == j, options[j], value)
    return value


def swapped(rows, mask, groups):
    block = rows.shape[0] // groups
    return jnp.concatenate(
        [rows[(j ^ mask) * block : ((j ^ mask) + 1) * block] for j in range(groups)], axis=0
    )


def doubled(matrix):
    return jnp.concatenate([matrix, matrix], axis=1)


def step_rows(parts, t):
    return jnp.concatenate([part[t] for part in parts], axis=0)


class Plan:
    def __init__(self, groups, share, dwell, owned, tracks, width):
        self.groups, self.share, self.dwell = groups, share, dwell
        self.owned, self.tracks, self.width = owned, tracks, width
        self.span, self.rows = share * dwell, groups * tracks
        self.extra = -(-share // tracks)
        self.spare = share // 4
        self.fast = share - self.spare

    def local(self, regime_ref, peer, b):
        return regime_ref[peer * self.share + b] - lax.axis_index("track") * self.owned

    def here(self, regime_ref, peer, b):
        return jnp.clip(self.local(regime_ref, peer, b), 0, self.owned - 1)

    def source(self, regime_ref, b):
        me = lax.axis_index("track")
        return (regime_ref[me * self.share + b] // self.owned) ^ me

    def gain_row(self, regime_ref, meas, b):
        step, row = self.span + b // self.tracks, b % self.tracks
        return choose(
            self.source(regime_ref, b), [part[step][row : row + 1] for part in meas]
        )

    def forward_steps(self):
        return [(b, b * self.dwell + i) for i in range(self.dwell) for b in range(self.share)]

    def backward_steps(self):
        turn = self.dwell - 1
        return [(b, t + turn - 2 * (t % self.dwell)) for b, t in self.forward_steps()]


def each_row(plan, regime_ref, table_ref, targets, sem, act):
    def row(held, at, target):
        @pl.when(held)
        def _():
            copy = pltpu.make_async_copy(table_ref.at[at], target, sem)
            copy.start() if act else copy.wait()

    for j, main, more in targets:
        peer = lax.axis_index("track") ^ j
        slot = jnp.int32(0)
        for b in range(plan.share):
            at = plan.local(regime_ref, peer, b)
            held = jnp.logical_and(at >= 0, at < plan.owned)
            if j == 0:
                row(held, at, main.at[b])
                continue
            if b < plan.fast:
                row(held, at, main.at[slot])
            else:
                fits = slot < plan.fast
                row(jnp.logical_and(held, fits), at, main.at[jnp.minimum(slot, plan.fast - 1)])
                late = jnp.clip(slot - plan.fast, 0, plan.spare - 1)
                row(jnp.logical_and(held, jnp.logical_not(fits)), at, more.at[late])
            slot = slot + held.astype(jnp.int32)


def remote_targets(plan, refs):
    peers = plan.groups - 1
    return [(j + 1, refs[j], refs[peers + j]) for j in range(peers)]


def gather_kernel(plan, regime_ref, table_ref, *refs):
    for act in (True, False):
        each_row(plan, regime_ref, table_ref, remote_targets(plan, refs[:-1]), refs[-1], act)


def second_gather_kernel(plan, regime_ref, first_ref, second_ref, *refs):
    own_first, own_second, refs, sem = (refs[0], refs[1], refs[2:-1], refs[-1])
    targets = [(0, own_second, None)] + remote_targets(plan, refs)
    for act in (True, False):
        each_row(plan, regime_ref, first_ref, [(0, own_first, None)], sem, act)
        each_row(plan, regime_ref, second_ref, targets, sem, act)


def picked_matrix(plan, regime_ref, refs, b):
    peers = plan.groups - 1
    own, main, more = (refs[0], refs[1 : peers + 1], refs[peers + 1 :])
    me = lax.axis_index("track")
    holder = [lax.div(regime_ref[me * plan.share + i], plan.owned) for i in range(b + 1)]
    slot = sum((holder[i] == holder[b]).astype(jnp.int32) for i in range(b)) if b else 0
    source = holder[b] ^ me
    if b < plan.fast:
        return choose(source, [own[b]] + [part[slot] for part in main])
    found = choose(source, [own[b]] + [part[jnp.minimum(slot, plan.fast - 1)] for part in main])
    late = jnp.clip(slot - plan.fast, 0, plan.spare - 1)
    rest = choose(source, [own[b]] + [part[late] for part in more])
    return jnp.where(slot < plan.fast, found, rest)


def measured_kernel(plan, regime_ref, gains_ref, obs_ref, *refs):
    meas, over_ref, gain_ref = (refs[:-2], refs[-2], refs[-1])
    gain_ref[...] = gains_ref[...].astype(F32)
    for j in range(plan.groups):
        peer = lax.axis_index("track") ^ j
        first = pl.multiple_of(peer * plan.span, plan.span)
        meas[j][0 : plan.span] = obs_ref[pl.ds(first, plan.span)]
        for e in range(plan.extra):
            blocks = [min(e * plan.tracks + i, plan.share - 1) for i in range(plan.tracks)]
            meas[j][plan.span + e] = jnp.concatenate(
                [gain_ref[pl.ds(plan.here(regime_ref, peer, b), 1), :] for b in blocks], axis=0
            )
    most = jnp.int32(0)
    for peer in range(plan.groups):
        holder = [lax.div(regime_ref[peer * plan.share + b], plan.owned) for b in range(plan.share)]
        for q in range(plan.groups):
            if q != peer:
                most = jnp.maximum(most, sum((at == q).astype(jnp.int32) for at in holder))
    over_ref[0] = most


def joined(charts):
    while len(charts) > 1:
        odd = charts[len(charts) // 2 * 2 :]
        charts = [compose(charts[i], charts[i + 1]) for i in range(0, len(charts) - 1, 2)] + odd
    return charts[0]


def running(charts):
    if len(charts) == 1:
        return charts
    pairs = running([compose(charts[i], charts[i + 1]) for i in range(0, len(charts) - 1, 2)])
    found = [charts[0]]
    for i in range(1, len(charts)):
        found.append(pairs[i // 2] if i % 2 else compose(pairs[i // 2 - 1], charts[i]))
    return found


def forward_kernel(plan, regime_ref, *refs):
    count = 2 * plan.groups - 1
    mats, meas = (refs[:count], refs[count : count + plan.groups])
    total_ref, strand_ref, picked_ref = refs[count + plan.groups :]
    weights, gains, states = ([], [], [])
    for b in range(plan.share):
        picked = picked_matrix(plan, regime_ref, mats, b)
        picked_ref[b] = picked
        weights.append(doubled(picked))
        gains.append(plan.gain_row(regime_ref, meas, b))
        driven = gains[b] * step_rows(meas, b * plan.dwell)
        kept = picked.astype(F32).T * (1.0 - gains[b])
        states.append(jnp.concatenate([kept, driven], axis=0))
    for b, t in plan.forward_steps():
        if t % plan.dwell == 0:
            continue
        kept = times_rows(states[b], weights[b]) * (1.0 - gains[b])
        driven = gains[b] * step_rows(meas, t)
        states[b] = jnp.concatenate(
            [kept[: plan.width], kept[plan.width :] + driven], axis=0
        )
    for b in range(plan.share):
        strand_ref[b] = states[b]
    total_ref[...] = joined(states)


def gain_levels(charts):
    found = [charts]
    while len(charts) > 1:
        charts = [times(charts[i], charts[i + 1]) for i in range(0, len(charts), 2)]
        found.append(charts)
    return found


def backward_kernel(plan, regime_ref, *refs):
    mats, (level_ref, picked_ref) = (refs[:-2], refs[-2:])
    weights, states = ([], [])
    for b in range(plan.share):
        picked = picked_matrix(plan, regime_ref, mats, b)
        picked_ref[b] = picked
        weights.append(doubled(picked))
        states.append(picked.astype(F32).T)
    for b, t in plan.backward_steps():
        if t % plan.dwell < plan.dwell - 1:
            states[b] = times_rows(states[b], weights[b])
    at = 0
    for level in gain_levels(states[::-1]):
        for chart in level:
            level_ref[at] = chart
            at += 1


def forward_running_kernel(strand_ref, running_ref):
    charts = [strand_ref[s] for s in range(strand_ref.shape[0] - 1)]
    for s, chart in enumerate(running(charts)):
        running_ref[s] = chart


def backward_running_kernel(level_ref, offset_ref, running_ref):
    charts = [
        jnp.concatenate([level_ref[s], offset_ref[s]], axis=0)
        for s in range(offset_ref.shape[0] - 1)
    ]
    for s, chart in enumerate(running(charts)):
        running_ref[s] = chart


def group_kernel(plan, reverse, *refs):
    groups, width = (plan.groups, plan.width)
    parts, (total_ref, before_ref) = (refs[:groups], refs[groups:])
    fixed = []
    for j in range(groups):
        part = parts[j][...]
        fixed.append(jnp.concatenate([part[:width], swapped(part[width:], j, groups)], axis=0))
    me = lax.axis_index("track")
    order = list(range(groups))[::-1] if reverse else list(range(groups))
    charts = [choose(me ^ q, fixed) for q in order]
    place = groups - 1 - me if reverse else me
    befores = [unit_chart(width, plan.rows), charts[0]]
    while len(befores) < groups:
        befores.append(compose(befores[-1], charts[len(befores) - 1]))
    before_ref[...] = choose(place, befores)
    total_ref[...] = joined(charts)


def is_second(mask, reverse):
    second = (lax.axis_index("tm") & mask) != 0
    return jnp.logical_not(second) if reverse else second


def pair_kernel(mask, reverse, last, own_ref, other_ref, before_ref, joined_ref, after_ref):
    width = own_ref.shape[1]
    own, other, before = (own_ref[...], other_ref[...], before_ref[...])
    second = is_second(mask, reverse)
    earlier, later = (jnp.where(second, other, own), jnp.where(second, own, other))
    if last:
        joined_ref[...] = apply(earlier[width:], later)
    else:
        joined_ref[...] = compose(earlier, later)
    after_ref[...] = jnp.where(second, compose(other, before), before)


def entering(far_ref, before_ref, running_ref, reverse):
    far = far_ref[...]
    second = is_second(lax.axis_size("tm") // 2, reverse)
    state = apply(jnp.where(second, far, jnp.zeros_like(far)), before_ref[...])
    return [state] + [apply(state, running_ref[s]) for s in range(running_ref.shape[0])]


def filter_kernel(plan, regime_ref, before_ref, far_ref, running_ref, fpick_ref, *refs):
    meas, refs = (refs[: plan.groups], refs[plan.groups :])
    level_ref, bpick_ref, filtered_ref, pushed_ref, offset_ref, total_ref = refs
    states = entering(far_ref, before_ref, running_ref, False)
    gains = [plan.gain_row(regime_ref, meas, b) for b in range(plan.share)]
    weights = [doubled(fpick_ref[b]) for b in range(plan.share)]
    pushes = {}
    for b, t in plan.forward_steps():
        ahead = times_rows(states[b], weights[b])
        pushes[t] = gains[b] * (step_rows(meas, t) - ahead)
        states[b] = ahead + pushes[t]
        filtered_ref[t] = states[b]
        pushed_ref[t] = pushes[t]
    weights = [doubled(bpick_ref[b]) for b in range(plan.share)]
    states = [None] * plan.share
    for b, t in plan.backward_steps():
        state = pushes[t] if states[b] is None else states[b] + pushes[t]
        states[b] = times_rows(state, weights[b])
    states = states[::-1]
    for b in range(plan.share):
        offset_ref[b] = states[b]
    at = 0
    while len(states) > 1:
        count = len(states)
        states = [
            times(states[i], level_ref[at + i + 1]) + states[i + 1] for i in range(0, count, 2)
        ]
        at += count
    total_ref[0 : plan.width] = level_ref[at]
    total_ref[plan.width :] = states[0]


def smooth_kernel(
    plan, before_ref, far_ref, running_ref, picked_ref, filtered_ref, pushed_ref, *outs
):
    tracks = plan.tracks
    states = entering(far_ref, before_ref, running_ref, True)[::-1]
    weights = [doubled(picked_ref[b]) for b in range(plan.share)]
    for b, t in plan.backward_steps():
        value = filtered_ref[t] + states[b]
        for j in range(plan.groups):
            outs[j][t] = value[j * tracks : (j + 1) * tracks]
        if t % plan.dwell > 0:
            states[b] = times_rows(states[b] + pushed_ref[t], weights[b])


def collect_kernel(plan, *refs):
    parts, out_ref = (refs[: plan.groups], refs[plan.groups])
    for j in range(plan.groups):
        first = pl.multiple_of((lax.axis_index("track") ^ j) * plan.span, plan.span)
        out_ref[pl.ds(first, plan.span)] = parts[j][...]


def body(observations, dynamics, smoother_gain, gains, regime):
    length, tracks, width = observations.shape
    blocks = regime.shape[0]
    groups, spans = (lax.axis_size("track"), lax.axis_size("tm"))
    owned = dynamics.shape[0]
    plan = Plan(groups, blocks // groups, length // blocks, owned, tracks, width)
    chart = shape((width + plan.rows, width))
    offset = shape((plan.rows, width))
    share = plan.share
    block_mats = lambda count: shape((count, width, width), BF16)
    unit = width * width * width
    regime, observations, dynamics, smoother_gain, gains = [
        pltpu.with_memory_space_constraint(value, pltpu.HBM)
        for value in (regime, observations, dynamics, smoother_gain, gains)
    ]

    def swap(value, mask, axis):
        pairs = [(source, source ^ mask) for source in range(lax.axis_size(axis))]
        return lax.ppermute(value, axis, pairs)

    def exchange(values):
        return [values[0]] + [swap(values[j], j, "track") for j in range(1, groups)]

    sem = pltpu.SemaphoreType.DMA
    peers = groups - 1
    slots = [block_mats(plan.fast)] * peers + [block_mats(plan.spare)] * peers
    trans = call(
        functools.partial(gather_kernel, plan), slots, [SMEM, HBM], unit, [sem]
    )(regime, dynamics)
    atrans = [swap(value, j + 1, "track") for j, value in enumerate(trans[:peers])]
    *meas, over = call(
        functools.partial(measured_kernel, plan),
        [shape((plan.span + plan.extra, tracks, width))] * groups + [shape((1,), jnp.int32)],
        [SMEM, VMEM, VMEM],
        unit,
        [pltpu.VMEM((owned, width), F32)],
        [VMEM] * groups + [SMEM],
    )(regime, gains, observations)
    meas = exchange(meas)
    own, gown, *smooth = call(
        functools.partial(second_gather_kernel, plan),
        [block_mats(share)] * 2 + slots,
        [SMEM, HBM, HBM],
        unit,
        [sem],
    )(regime, dynamics, smoother_gain)

    def all_further(values):
        return [swap(value, j % peers + 1, "track") for j, value in enumerate(values)]

    further = lax.cond(
        over[0] > plan.fast, all_further, lambda values: values, [*trans[peers:], *smooth[peers:]]
    )
    total, fstrand, fpick = call(
        functools.partial(forward_kernel, plan),
        [chart, shape((share,) + chart.shape), block_mats(share)],
        [SMEM] + [VMEM] * (3 * groups - 1),
        400 * unit,
    )(regime, own, *atrans, *further[:peers], *meas)

    late, total = lax.optimization_barrier((smooth[:peers], total))

    def spread(total):
        return exchange([total] * groups)

    def across(total, reverse):
        maps = spread(total)
        total, before = call(
            functools.partial(group_kernel, plan, reverse),
            [chart, chart],
            [VMEM] * groups,
            20 * unit,
        )(*maps)
        stride = 1
        while 2 * stride < spans:
            last = 4 * stride >= spans
            total, before = call(
                functools.partial(pair_kernel, stride, reverse, last),
                [offset if last else chart, chart],
                [VMEM] * 3,
                20 * unit,
            )(total, swap(total, stride, "tm"), before)
            stride *= 2
        total = total[-plan.rows :] if stride == 1 else total
        return before, swap(total, stride, "tm")

    late = [swap(value, j + 1, "track") for j, value in enumerate(late)]
    levels = 2 * share - 1
    level, bpick = call(
        functools.partial(backward_kernel, plan),
        [shape((levels, width, width)), block_mats(share)],
        [SMEM] + [VMEM] * (2 * groups - 1),
        300 * unit,
    )(regime, gown, *late, *further[peers:])

    before, far = across(total, False)
    runs = [shape((share - 1,) + chart.shape)]
    (frun,) = call(forward_running_kernel, runs, [VMEM], 60 * unit)(fstrand)
    filtered, pushed, offsets, total = call(
        functools.partial(filter_kernel, plan),
        [shape((plan.span, plan.rows, width))] * 2 + [shape((share,) + offset.shape), chart],
        [SMEM] + [VMEM] * (6 + groups),
        100 * unit,
    )(regime, before, far, frun, fpick, *meas, level, bpick)

    before, far = across(total, True)
    (brun,) = call(backward_running_kernel, runs, [VMEM] * 2, 60 * unit)(level, offsets)
    outs = call(
        functools.partial(smooth_kernel, plan),
        [shape((plan.span, tracks, width))] * groups,
        [VMEM] * 6,
        50 * unit,
    )(before, far, brun, bpick, filtered, pushed)
    return call(
        functools.partial(collect_kernel, plan),
        [shape((length, tracks, width))],
        [VMEM] * groups,
        unit,
    )(*exchange(outs))[0]


def solution(mesh):
    placed = (
        P("tm", "track", None),
        P("track", None, None),
        P("track", None, None),
        P("track", None),
        P("tm"),
    )

    return jax.shard_map(
        body, mesh=mesh, in_specs=placed, out_specs=P("tm", "track", None), check_vma=False
    )
```

```python
import functools

import jax
import jax.numpy as jnp
from jax import lax
from jax.experimental import pallas as pl
from jax.experimental.pallas import tpu as pltpu
from jax.sharding import PartitionSpec as P


F32 = jnp.float32
BF16 = jnp.bfloat16
VMEM = pl.BlockSpec(memory_space=pltpu.VMEM)
SMEM = pl.BlockSpec(memory_space=pltpu.SMEM)
HBM = pl.BlockSpec(memory_space=pltpu.HBM)
GRANT = 16 * 1024 * 1024


def call(kernel, outs, ins, cost, scratch=(), places=None):
    return pl.pallas_call(
        kernel,
        out_shape=outs,
        in_specs=ins,
        out_specs=places or [VMEM] * len(outs),
        scratch_shapes=list(scratch),
        compiler_params=pltpu.CompilerParams(vmem_limit_bytes=GRANT),
        cost_estimate=pl.CostEstimate(flops=cost, bytes_accessed=cost // 64, transcendentals=0),
    )


def shape(dims, dtype=F32):
    return jax.ShapeDtypeStruct(dims, dtype)


def split(value):
    high = value.astype(BF16)
    low = (value - high.astype(F32)).astype(BF16)
    return high, low


def times_rows(value, doubled):
    pieces = jnp.concatenate(split(value), axis=1)
    return lax.dot_general(
        pieces, doubled, (((1,), (1,)), ((), ())), preferred_element_type=F32
    )


def times(value, matrix):
    high, low = split(value)
    upper, lower = split(matrix)
    left = jnp.concatenate([high, low, high], axis=1)
    right = jnp.concatenate([upper, upper, lower], axis=0)
    return jnp.dot(left, right, preferred_element_type=F32)


def compose(first, second):
    width = first.shape[1]
    product = times(first, second[:width])
    return jnp.concatenate([product[:width], product[width:] + second[width:]], axis=0)


def apply(state, chart):
    width = chart.shape[1]
    return times(state, chart[:width]) + chart[width:]


def unit_matrix(width):
    rows = lax.broadcasted_iota(jnp.int32, (width, width), 0)
    return (rows == lax.broadcasted_iota(jnp.int32, (width, width), 1)).astype(F32)


def unit_chart(width, rows):
    return jnp.concatenate([unit_matrix(width), jnp.zeros((rows, width), F32)], axis=0)


def choose(index, options):
    value = options[0]
    for j in range(1, len(options)):
        value = jnp.where(index == j, options[j], value)
    return value


def swapped(rows, mask, groups):
    block = rows.shape[0] // groups
    return jnp.concatenate(
        [rows[(j ^ mask) * block : ((j ^ mask) + 1) * block] for j in range(groups)], axis=0
    )


def doubled(matrix):
    return jnp.concatenate([matrix, matrix], axis=1)


def step_rows(parts, t):
    return jnp.concatenate([part[t] for part in parts], axis=0)


class Plan:
    def __init__(self, groups, share, dwell, owned, tracks, width):
        self.groups, self.share, self.dwell = groups, share, dwell
        self.owned, self.tracks, self.width = owned, tracks, width
        self.span, self.rows = share * dwell, groups * tracks
        self.extra = -(-share // tracks)
        self.spare = share // 4
        self.fast = share - self.spare

    def local(self, regime_ref, peer, b):
        return regime_ref[peer * self.share + b] - lax.axis_index("track") * self.owned

    def here(self, regime_ref, peer, b):
        return jnp.clip(self.local(regime_ref, peer, b), 0, self.owned - 1)

    def source(self, regime_ref, b):
        me = lax.axis_index("track")
        return (regime_ref[me * self.share + b] // self.owned) ^ me

    def gain_row(self, regime_ref, meas, b):
        step, row = self.span + b // self.tracks, b % self.tracks
        return choose(
            self.source(regime_ref, b), [part[step][row : row + 1] for part in meas]
        )

    def forward_steps(self):
        return [(b, b * self.dwell + i) for i in range(self.dwell) for b in range(self.share)]

    def backward_steps(self):
        turn = self.dwell - 1
        return [(b, t + turn - 2 * (t % self.dwell)) for b, t in self.forward_steps()]


def each_row(plan, regime_ref, table_ref, targets, sem, act):
    def row(held, at, target):
        @pl.when(held)
        def _():
            copy = pltpu.make_async_copy(table_ref.at[at], target, sem)
            copy.start() if act else copy.wait()

    for j, main, more in targets:
        peer = lax.axis_index("track") ^ j
        slot = jnp.int32(0)
        for b in range(plan.share):
            at = plan.local(regime_ref, peer, b)
            held = jnp.logical_and(at >= 0, at < plan.owned)
            if j == 0:
                row(held, at, main.at[b])
                continue
            if b < plan.fast:
                row(held, at, main.at[slot])
            else:
                fits = slot < plan.fast
                row(jnp.logical_and(held, fits), at, main.at[jnp.minimum(slot, plan.fast - 1)])
                late = jnp.clip(slot - plan.fast, 0, plan.spare - 1)
                row(jnp.logical_and(held, jnp.logical_not(fits)), at, more.at[late])
            slot = slot + held.astype(jnp.int32)


def remote_targets(plan, refs):
    peers = plan.groups - 1
    return [(j + 1, refs[j], refs[peers + j]) for j in range(peers)]


def gather_kernel(plan, regime_ref, table_ref, *refs):
    for act in (True, False):
        each_row(plan, regime_ref, table_ref, remote_targets(plan, refs[:-1]), refs[-1], act)


def second_gather_kernel(plan, regime_ref, first_ref, second_ref, *refs):
    own_first, own_second, refs, sem = (refs[0], refs[1], refs[2:-1], refs[-1])
    targets = [(0, own_second, None)] + remote_targets(plan, refs)
    for act in (True, False):
        each_row(plan, regime_ref, first_ref, [(0, own_first, None)], sem, act)
        each_row(plan, regime_ref, second_ref, targets, sem, act)


def picked_matrix(plan, regime_ref, refs, b):
    peers = plan.groups - 1
    own, main, more = (refs[0], refs[1 : peers + 1], refs[peers + 1 :])
    me = lax.axis_index("track")
    holder = [lax.div(regime_ref[me * plan.share + i], plan.owned) for i in range(b + 1)]
    slot = sum((holder[i] == holder[b]).astype(jnp.int32) for i in range(b)) if b else 0
    source = holder[b] ^ me
    if b < plan.fast:
        return choose(source, [own[b]] + [part[slot] for part in main])
    found = choose(source, [own[b]] + [part[jnp.minimum(slot, plan.fast - 1)] for part in main])
    late = jnp.clip(slot - plan.fast, 0, plan.spare - 1)
    rest = choose(source, [own[b]] + [part[late] for part in more])
    return jnp.where(slot < plan.fast, found, rest)


def measured_kernel(plan, regime_ref, gains_ref, obs_ref, *refs):
    meas, over_ref, gain_ref = (refs[:-2], refs[-2], refs[-1])
    gain_ref[...] = gains_ref[...].astype(F32)
    for j in range(plan.groups):
        peer = lax.axis_index("track") ^ j
        first = pl.multiple_of(peer * plan.span, plan.span)
        meas[j][0 : plan.span] = obs_ref[pl.ds(first, plan.span)]
        for e in range(plan.extra):
            blocks = [min(e * plan.tracks + i, plan.share - 1) for i in range(plan.tracks)]
            meas[j][plan.span + e] = jnp.concatenate(
                [gain_ref[pl.ds(plan.here(regime_ref, peer, b), 1), :] for b in blocks], axis=0
            )
    most = jnp.int32(0)
    for peer in range(plan.groups):
        holder = [lax.div(regime_ref[peer * plan.share + b], plan.owned) for b in range(plan.share)]
        for q in range(plan.groups):
            if q != peer:
                most = jnp.maximum(most, sum((at == q).astype(jnp.int32) for at in holder))
    over_ref[0] = most


def joined(charts):
    while len(charts) > 1:
        odd = charts[len(charts) // 2 * 2 :]
        charts = [compose(charts[i], charts[i + 1]) for i in range(0, len(charts) - 1, 2)] + odd
    return charts[0]


def running(charts):
    if len(charts) == 1:
        return charts
    pairs = running([compose(charts[i], charts[i + 1]) for i in range(0, len(charts) - 1, 2)])
    found = [charts[0]]
    for i in range(1, len(charts)):
        found.append(pairs[i // 2] if i % 2 else compose(pairs[i // 2 - 1], charts[i]))
    return found


def forward_kernel(plan, regime_ref, *refs):
    count = 2 * plan.groups - 1
    mats, meas = (refs[:count], refs[count : count + plan.groups])
    total_ref, strand_ref, picked_ref = refs[count + plan.groups :]
    weights, gains, states = ([], [], [])
    for b in range(plan.share):
        picked = picked_matrix(plan, regime_ref, mats, b)
        picked_ref[b] = picked
        weights.append(doubled(picked))
        gains.append(plan.gain_row(regime_ref, meas, b))
        driven = gains[b] * step_rows(meas, b * plan.dwell)
        kept = picked.astype(F32).T * (1.0 - gains[b])
        states.append(jnp.concatenate([kept, driven], axis=0))
    for b, t in plan.forward_steps():
        if t % plan.dwell == 0:
            continue
        kept = times_rows(states[b], weights[b]) * (1.0 - gains[b])
        driven = gains[b] * step_rows(meas, t)
        states[b] = jnp.concatenate(
            [kept[: plan.width], kept[plan.width :] + driven], axis=0
        )
    for b in range(plan.share):
        strand_ref[b] = states[b]
    total_ref[...] = joined(states)


def backward_kernel(plan, regime_ref, *refs):
    mats, (strand_ref, picked_ref) = (refs[:-2], refs[-2:])
    weights, states = ([], [])
    for b in range(plan.share):
        picked = picked_matrix(plan, regime_ref, mats, b)
        picked_ref[b] = picked
        weights.append(doubled(picked))
        states.append(picked.astype(F32).T)
    for b, t in plan.backward_steps():
        if t % plan.dwell < plan.dwell - 1:
            states[b] = times_rows(states[b], weights[b])
    for b in range(plan.share):
        strand_ref[b] = states[plan.share - 1 - b]


def forward_running_kernel(strand_ref, running_ref):
    charts = [strand_ref[s] for s in range(strand_ref.shape[0] - 1)]
    for s, chart in enumerate(running(charts)):
        running_ref[s] = chart


def backward_running_kernel(strand_ref, offset_ref, running_ref):
    charts = [
        jnp.concatenate([strand_ref[s], offset_ref[s]], axis=0)
        for s in range(offset_ref.shape[0] - 1)
    ]
    for s, chart in enumerate(running(charts)):
        running_ref[s] = chart


def group_kernel(plan, reverse, *refs):
    groups, width = (plan.groups, plan.width)
    parts, (total_ref, before_ref) = (refs[:groups], refs[groups:])
    fixed = []
    for j in range(groups):
        part = parts[j][...]
        fixed.append(jnp.concatenate([part[:width], swapped(part[width:], j, groups)], axis=0))
    me = lax.axis_index("track")
    order = list(range(groups))[::-1] if reverse else list(range(groups))
    charts = [choose(me ^ q, fixed) for q in order]
    place = groups - 1 - me if reverse else me
    befores = [unit_chart(width, plan.rows), charts[0]]
    while len(befores) < groups:
        befores.append(compose(befores[-1], charts[len(befores) - 1]))
    before_ref[...] = choose(place, befores)
    total_ref[...] = joined(charts)


def is_second(mask, reverse):
    second = (lax.axis_index("tm") & mask) != 0
    return jnp.logical_not(second) if reverse else second


def pair_kernel(mask, reverse, own_ref, other_ref, before_ref, joined_ref, after_ref, *half_ref):
    own, other, before = (own_ref[...], other_ref[...], before_ref[...])
    second = is_second(mask, reverse)
    joined = compose(jnp.where(second, other, own), jnp.where(second, own, other))
    joined_ref[...] = joined
    after_ref[...] = jnp.where(second, compose(other, before), before)
    if half_ref:
        rows = joined.shape[0] // 2
        half_ref[0][...] = jnp.where(is_second(1, False), joined[rows:], joined[:rows])


def entering(found, running_ref, stride, reverse):
    before_ref, mine_ref, theirs_ref, half_ref, rest_ref = found
    odd = is_second(1, False)
    mine, theirs, half, rest = (mine_ref[...], theirs_ref[...], half_ref[...], rest_ref[...])
    across = jnp.concatenate([jnp.where(odd, rest, half), jnp.where(odd, half, rest)], axis=0)
    peers = [mine, jnp.where(odd, theirs, mine), jnp.where(odd, mine, theirs), across]
    low, high = (is_second(stride, False), is_second(2 * stride, False))
    quarter = low.astype(jnp.int32) + 2 * high.astype(jnp.int32)
    width = mine.shape[1]
    state = None
    for at in (3, 2, 1) if reverse else (0, 1, 2):
        chart = choose(quarter ^ at, peers)
        ahead = quarter < at if reverse else quarter > at
        if state is None:
            state = jnp.where(ahead, chart[width:], jnp.zeros_like(chart[width:]))
        else:
            state = jnp.where(ahead, apply(state, chart), state)
    state = apply(state, before_ref[...])
    return [state] + [apply(state, running_ref[s]) for s in range(running_ref.shape[0])]


def filter_kernel(plan, stride, regime_ref, *refs):
    found, (running_ref, fpick_ref), refs = (refs[:5], refs[5:7], refs[7:])
    meas, refs = (refs[: plan.groups], refs[plan.groups :])
    strand_ref, bpick_ref, filtered_ref, pushed_ref, offset_ref, total_ref = refs
    states = entering(found, running_ref, stride, False)
    gains = [plan.gain_row(regime_ref, meas, b) for b in range(plan.share)]
    weights = [doubled(fpick_ref[b]) for b in range(plan.share)]
    pushes = {}
    for b, t in plan.forward_steps():
        ahead = times_rows(states[b], weights[b])
        pushes[t] = gains[b] * (step_rows(meas, t) - ahead)
        states[b] = ahead + pushes[t]
        filtered_ref[t] = states[b]
        pushed_ref[t] = pushes[t]
    weights = [doubled(bpick_ref[b]) for b in range(plan.share)]
    states = [None] * plan.share
    for b, t in plan.backward_steps():
        state = pushes[t] if states[b] is None else states[b] + pushes[t]
        states[b] = times_rows(state, weights[b])
    states = states[::-1]
    for b in range(plan.share):
        offset_ref[b] = states[b]
    mats = [strand_ref[b] for b in range(plan.share)]
    while len(states) > 1:
        pairs = range(0, len(states), 2)
        states = [times(states[i], mats[i + 1]) + states[i + 1] for i in pairs]
        mats = [times(mats[i], mats[i + 1]) for i in pairs]
    total_ref[0 : plan.width] = mats[0]
    total_ref[plan.width :] = states[0]


def smooth_kernel(plan, stride, *refs):
    found, (running_ref, picked_ref, filtered_ref, pushed_ref), outs = (refs[:5], refs[5:9], refs[9:])
    tracks = plan.tracks
    states = entering(found, running_ref, stride, True)[::-1]
    weights = [doubled(picked_ref[b]) for b in range(plan.share)]
    for b, t in plan.backward_steps():
        value = filtered_ref[t] + states[b]
        for j in range(plan.groups):
            outs[j][t] = value[j * tracks : (j + 1) * tracks]
        if t % plan.dwell > 0:
            states[b] = times_rows(states[b] + pushed_ref[t], weights[b])


def collect_kernel(plan, *refs):
    parts, out_ref, sem = (refs[: plan.groups], refs[plan.groups], refs[plan.groups + 1])
    copies = []
    for j in range(plan.groups):
        first = pl.multiple_of((lax.axis_index("track") ^ j) * plan.span, plan.span)
        rows = out_ref.at[pl.ds(first, plan.span)]
        copies.append(pltpu.make_async_copy(parts[j], rows, sem.at[j]))
    for copy in copies:
        copy.start()
    for copy in copies:
        copy.wait()


def body(observations, dynamics, smoother_gain, gains, regime):
    length, tracks, width = observations.shape
    blocks = regime.shape[0]
    groups, spans = (lax.axis_size("track"), lax.axis_size("tm"))
    owned = dynamics.shape[0]
    plan = Plan(groups, blocks // groups, length // blocks, owned, tracks, width)
    chart = shape((width + plan.rows, width))
    offset = shape((plan.rows, width))
    half_chart = shape(((width + plan.rows) // 2, width))
    top = spans // 4
    share = plan.share
    block_mats = lambda count: shape((count, width, width), BF16)
    unit = width * width * width
    regime, observations, dynamics, smoother_gain, gains = [
        pltpu.with_memory_space_constraint(value, pltpu.HBM)
        for value in (regime, observations, dynamics, smoother_gain, gains)
    ]

    def swap(value, mask, axis):
        pairs = [(source, source ^ mask) for source in range(lax.axis_size(axis))]
        return lax.ppermute(value, axis, pairs)

    def exchange(values):
        return [values[0]] + [swap(values[j], j, "track") for j in range(1, groups)]

    sem = pltpu.SemaphoreType.DMA
    peers = groups - 1
    slots = [block_mats(plan.fast)] * peers + [block_mats(plan.spare)] * peers
    trans = call(
        functools.partial(gather_kernel, plan), slots, [SMEM, HBM], unit, [sem]
    )(regime, dynamics)
    atrans = [swap(value, j + 1, "track") for j, value in enumerate(trans[:peers])]
    *meas, over = call(
        functools.partial(measured_kernel, plan),
        [shape((plan.span + plan.extra, tracks, width))] * groups + [shape((1,), jnp.int32)],
        [SMEM, VMEM, VMEM],
        unit,
        [pltpu.VMEM((owned, width), F32)],
        [VMEM] * groups + [SMEM],
    )(regime, gains, observations)
    meas = exchange(meas)
    own, gown, *smooth = call(
        functools.partial(second_gather_kernel, plan),
        [block_mats(share)] * 2 + slots,
        [SMEM, HBM, HBM],
        unit,
        [sem],
    )(regime, dynamics, smoother_gain)

    def all_further(values):
        return [swap(value, j % peers + 1, "track") for j, value in enumerate(values)]

    further = lax.cond(
        over[0] > plan.fast, all_further, lambda values: values, [*trans[peers:], *smooth[peers:]]
    )
    total, fstrand, fpick = call(
        functools.partial(forward_kernel, plan),
        [chart, shape((share,) + chart.shape), block_mats(share)],
        [SMEM] + [VMEM] * (3 * groups - 1),
        400 * unit,
    )(regime, own, *atrans, *further[:peers], *meas)

    late, total = lax.optimization_barrier((smooth[:peers], total))

    def spread(total):
        return exchange([total] * groups)

    def across(total, reverse):
        maps = spread(total)
        total, before = call(
            functools.partial(group_kernel, plan, reverse),
            [chart, chart],
            [VMEM] * groups,
            20 * unit,
        )(*maps)
        stride = 1
        while 4 * stride < spans:
            last = 8 * stride >= spans
            other = swap(total, stride, "tm")
            total, before, *half = call(
                functools.partial(pair_kernel, stride, reverse),
                [chart, chart] + [half_chart] * last,
                [VMEM] * 3,
                20 * unit,
            )(total, other, before)
            stride *= 2
        near = [(at, at ^ (stride << (at & 1))) for at in range(spans)]
        mine = lax.ppermute(total, "tm", near)
        half = swap(half[0], 3 * stride, "tm")
        theirs = swap(mine, 1, "tm")
        return before, mine, theirs, half, swap(half, 1, "tm")

    for j, value in enumerate(late):
        late[j] = swap(value, j + 1, "track")
    bstrand, bpick = call(
        functools.partial(backward_kernel, plan),
        [shape((share, width, width)), block_mats(share)],
        [SMEM] + [VMEM] * (2 * groups - 1),
        300 * unit,
    )(regime, gown, *late, *further[peers:])

    found = across(total, False)
    runs = [shape((share - 1,) + chart.shape)]
    (frun,) = call(forward_running_kernel, runs, [VMEM], 60 * unit)(fstrand)
    filtered, pushed, offsets, total = call(
        functools.partial(filter_kernel, plan, top),
        [shape((plan.span, plan.rows, width))] * 2 + [shape((share,) + offset.shape), chart],
        [SMEM] + [VMEM] * (9 + groups),
        100 * unit,
    )(regime, *found, frun, fpick, *meas, bstrand, bpick)

    found = across(total, True)
    (brun,) = call(backward_running_kernel, runs, [VMEM] * 2, 60 * unit)(bstrand, offsets)
    outs = call(
        functools.partial(smooth_kernel, plan, top),
        [shape((plan.span, tracks, width))] * groups,
        [VMEM] * 9,
        50 * unit,
    )(*found, brun, bpick, filtered, pushed)
    return call(
        functools.partial(collect_kernel, plan),
        [shape((length, tracks, width))],
        [VMEM] * groups,
        unit,
        [sem((groups,))],
        [HBM],
    )(*exchange(outs))[0]


def solution(mesh):
    placed = (
        P("tm", "track", None),
        P("track", None, None),
        P("track", None, None),
        P("track", None),
        P("tm"),
    )

    return jax.shard_map(
        body, mesh=mesh, in_specs=placed, out_specs=P("tm", "track", None), check_vma=False
    )
```

```python
import functools

import jax
import jax.numpy as jnp
from jax import lax
from jax.experimental import pallas as pl
from jax.experimental.pallas import tpu as pltpu
from jax.sharding import PartitionSpec as P


F32 = jnp.float32
BF16 = jnp.bfloat16
VMEM = pl.BlockSpec(memory_space=pltpu.VMEM)
SMEM = pl.BlockSpec(memory_space=pltpu.SMEM)
HBM = pl.BlockSpec(memory_space=pltpu.HBM)
GRANT = 16 * 1024 * 1024


def call(kernel, outs, ins, cost, scratch=(), places=None):
    return pl.pallas_call(
        kernel,
        out_shape=outs,
        in_specs=ins,
        out_specs=places or [VMEM] * len(outs),
        scratch_shapes=list(scratch),
        compiler_params=pltpu.CompilerParams(vmem_limit_bytes=GRANT),
        cost_estimate=pl.CostEstimate(flops=cost, bytes_accessed=cost // 64, transcendentals=0),
    )


def shape(dims, dtype=F32):
    return jax.ShapeDtypeStruct(dims, dtype)


def split(value):
    high = value.astype(BF16)
    low = (value - high.astype(F32)).astype(BF16)
    return high, low


def times_rows(value, doubled):
    pieces = jnp.concatenate(split(value), axis=1)
    return lax.dot_general(
        pieces, doubled, (((1,), (1,)), ((), ())), preferred_element_type=F32
    )


def times(value, matrix):
    high, low = split(value)
    upper, lower = split(matrix)
    left = jnp.concatenate([high, low, high], axis=1)
    right = jnp.concatenate([upper, upper, lower], axis=0)
    return jnp.dot(left, right, preferred_element_type=F32)


def compose(first, second):
    width = first.shape[1]
    product = times(first, second[:width])
    return jnp.concatenate([product[:width], product[width:] + second[width:]], axis=0)


def apply(state, chart):
    width = chart.shape[1]
    return times(state, chart[:width]) + chart[width:]


def unit_matrix(width):
    rows = lax.broadcasted_iota(jnp.int32, (width, width), 0)
    return (rows == lax.broadcasted_iota(jnp.int32, (width, width), 1)).astype(F32)


def unit_chart(width, rows):
    return jnp.concatenate([unit_matrix(width), jnp.zeros((rows, width), F32)], axis=0)


def choose(index, options):
    value = options[0]
    for j in range(1, len(options)):
        value = jnp.where(index == j, options[j], value)
    return value


def swapped(rows, mask, groups):
    block = rows.shape[0] // groups
    return jnp.concatenate(
        [rows[(j ^ mask) * block : ((j ^ mask) + 1) * block] for j in range(groups)], axis=0
    )


def doubled(matrix):
    return jnp.concatenate([matrix, matrix], axis=1)


def step_rows(parts, t):
    return jnp.concatenate([part[t] for part in parts], axis=0)


class Plan:
    def __init__(self, groups, share, dwell, owned, tracks, width):
        self.groups, self.share, self.dwell = groups, share, dwell
        self.owned, self.tracks, self.width = owned, tracks, width
        self.span, self.rows = share * dwell, groups * tracks
        self.padded = -(-share // 16) * 16
        self.spare = share // 4
        self.fast = share - self.spare

    def local(self, regime_ref, peer, b):
        return regime_ref[peer * self.share + b] - lax.axis_index("track") * self.owned

    def here(self, regime_ref, peer, b):
        return jnp.clip(self.local(regime_ref, peer, b), 0, self.owned - 1)

    def source(self, regime_ref, b):
        me = lax.axis_index("track")
        return (regime_ref[me * self.share + b] // self.owned) ^ me

    def forward_steps(self):
        return [(b, b * self.dwell + i) for i in range(self.dwell) for b in range(self.share)]

    def backward_steps(self):
        turn = self.dwell - 1
        return [(b, t + turn - 2 * (t % self.dwell)) for b, t in self.forward_steps()]


def block_of(plan, ref, at):
    return ref.at[pl.ds(pl.multiple_of(at * plan.width, plan.width), plan.width)]


def each_row(plan, regime_ref, table_ref, targets, sem, act):
    def row(held, at, target):
        @pl.when(held)
        def _():
            copy = pltpu.make_async_copy(table_ref.at[at], target, sem)
            copy.start() if act else copy.wait()

    for j, main, more in targets:
        peer = lax.axis_index("track") ^ j
        slot = jnp.int32(0)
        for b in range(plan.share):
            at = plan.local(regime_ref, peer, b)
            held = jnp.logical_and(at >= 0, at < plan.owned)
            at = jnp.clip(at, 0, plan.owned - 1)
            if j == 0:
                row(held, at, block_of(plan, main, b))
                continue
            if b < plan.fast:
                row(held, at, block_of(plan, main, slot))
            else:
                fits = slot < plan.fast
                room = jnp.minimum(slot, plan.fast - 1)
                row(jnp.logical_and(held, fits), at, block_of(plan, main, room))
                late = jnp.clip(slot - plan.fast, 0, plan.spare - 1)
                row(jnp.logical_and(held, jnp.logical_not(fits)), at, block_of(plan, more, late))
            slot = slot + held.astype(jnp.int32)


def remote_targets(plan, refs):
    peers = plan.groups - 1
    return [(j + 1, refs[j], refs[peers + j]) for j in range(peers)]


def gather_kernel(plan, regime_ref, table_ref, gains_ref, *refs):
    own_ref, refs, (gain_ref, sem) = (refs[0], refs[1:-2], refs[-2:])
    each_row(plan, regime_ref, table_ref, remote_targets(plan, refs), sem, True)
    gain_ref[...] = gains_ref[...].astype(F32)
    for j in range(plan.groups):
        peer = lax.axis_index("track") ^ j
        rows = [min(b, plan.share - 1) for b in range(plan.padded)]
        found = [gain_ref[pl.ds(plan.here(regime_ref, peer, b), 1), :] for b in range(plan.share)]
        tile = jnp.concatenate([found[b] for b in rows], axis=0).astype(BF16)
        if j:
            refs[j - 1][plan.fast * plan.width :] = tile
        else:
            own_ref[...] = tile
    each_row(plan, regime_ref, table_ref, remote_targets(plan, refs), sem, False)


def second_gather_kernel(plan, regime_ref, first_ref, second_ref, *refs):
    over_ref, own_first, own_second, refs, sem = (*refs[:3], refs[3:-1], refs[-1])
    targets = [(0, own_second, None)] + remote_targets(plan, refs)
    for act in (True, False):
        each_row(plan, regime_ref, first_ref, [(0, own_first, None)], sem, act)
        each_row(plan, regime_ref, second_ref, targets, sem, act)
        if act:
            over_ref[0] = most_slots(plan, regime_ref)


def picked_matrix(plan, regime_ref, refs, b):
    peers = plan.groups - 1
    own, main, more = (refs[0], refs[1 : peers + 1], refs[peers + 1 :])
    me = lax.axis_index("track")
    holder = [lax.div(regime_ref[me * plan.share + i], plan.owned) for i in range(b + 1)]
    slot = sum((holder[i] == holder[b]).astype(jnp.int32) for i in range(b)) if b else 0
    source = holder[b] ^ me
    mine = own[b * plan.width : (b + 1) * plan.width]
    if b < plan.fast:
        return choose(source, [mine] + [block_of(plan, part, slot)[...] for part in main])
    room = jnp.minimum(slot, plan.fast - 1)
    found = choose(source, [mine] + [block_of(plan, part, room)[...] for part in main])
    late = jnp.clip(slot - plan.fast, 0, plan.spare - 1)
    rest = choose(source, [mine] + [block_of(plan, part, late)[...] for part in more])
    return jnp.where(slot < plan.fast, found, rest)


def measured_kernel(plan, obs_ref, *refs):
    meas, sem = (refs[:-1], refs[-1])
    copies = []
    for j in range(plan.groups):
        first = pl.multiple_of((lax.axis_index("track") ^ j) * plan.span, plan.span)
        rows = obs_ref.at[pl.ds(first, plan.span)]
        copies.append(pltpu.make_async_copy(rows, meas[j], sem.at[j]))
    for copy in copies:
        copy.start()
    for copy in copies:
        copy.wait()


def most_slots(plan, regime_ref):
    most = jnp.int32(0)
    for peer in range(plan.groups):
        holder = [lax.div(regime_ref[peer * plan.share + b], plan.owned) for b in range(plan.share)]
        for q in range(plan.groups):
            if q != peer:
                most = jnp.maximum(most, sum((at == q).astype(jnp.int32) for at in holder))
    return most


def joined(charts):
    while len(charts) > 1:
        odd = charts[len(charts) // 2 * 2 :]
        charts = [compose(charts[i], charts[i + 1]) for i in range(0, len(charts) - 1, 2)] + odd
    return charts[0]


def running(charts):
    if len(charts) == 1:
        return charts
    pairs = running([compose(charts[i], charts[i + 1]) for i in range(0, len(charts) - 1, 2)])
    found = [charts[0]]
    for i in range(1, len(charts)):
        found.append(pairs[i // 2] if i % 2 else compose(pairs[i // 2 - 1], charts[i]))
    return found


def forward_kernel(plan, regime_ref, own_gain_ref, *refs):
    mats, (strand_ref, tree_ref, picked_ref, gain_ref) = (refs[:-4], refs[-4:])
    tiles = [own_gain_ref[...].astype(F32)]
    tiles += [part[plan.fast * plan.width :].astype(F32) for part in mats[1 : plan.groups]]
    weights, gains, states = ([], [], [])
    for b in range(plan.share):
        picked = picked_matrix(plan, regime_ref, mats, b)
        picked_ref[b] = picked
        weights.append(doubled(picked))
        source = plan.source(regime_ref, b)
        gains.append(choose(source, [tile[b : b + 1] for tile in tiles]))
        gain_ref[b : b + 1] = gains[b]
        states.append(picked.astype(F32).T * (1.0 - gains[b]))
    for b, t in plan.forward_steps():
        if t % plan.dwell > 0:
            states[b] = times_rows(states[b], weights[b]) * (1.0 - gains[b])
    for b in range(plan.share):
        strand_ref[b] = states[b]
    at = 0
    while len(states) > 1:
        states = [times(states[i], states[i + 1]) for i in range(0, len(states), 2)]
        for state in states:
            tree_ref[at] = state
            at += 1


def offset_kernel(plan, strand_ref, tree_ref, picked_ref, gain_ref, *refs):
    meas, (total_ref, offset_ref) = (refs[:-2], refs[-2:])
    gains = [gain_ref[b : b + 1] for b in range(plan.share)]
    weights = [doubled(picked_ref[b]) for b in range(plan.share)]
    states = [gains[b] * step_rows(meas, b * plan.dwell) for b in range(plan.share)]
    for b, t in plan.forward_steps():
        if t % plan.dwell > 0:
            moved = times_rows(states[b], weights[b]) * (1.0 - gains[b])
            states[b] = moved + gains[b] * step_rows(meas, t)
    for b in range(plan.share):
        offset_ref[b] = states[b]
    mats = [strand_ref[b] for b in range(plan.share)]
    at = 0
    while len(states) > 1:
        pairs = range(0, len(states), 2)
        states = [times(states[i], mats[i + 1]) + states[i + 1] for i in pairs]
        mats = [tree_ref[at + i] for i in range(len(states))]
        at += len(states)
    total_ref[: plan.width] = mats[0]
    total_ref[plan.width :] = states[0]


def backward_kernel(plan, regime_ref, *refs):
    mats, (strand_ref, picked_ref) = (refs[:-2], refs[-2:])
    weights, states = ([], [])
    for b in range(plan.share):
        picked = picked_matrix(plan, regime_ref, mats, b)
        picked_ref[b] = picked
        weights.append(doubled(picked))
        states.append(picked.astype(F32).T)
    for b, t in plan.backward_steps():
        if t % plan.dwell < plan.dwell - 1:
            states[b] = times_rows(states[b], weights[b])
    for b in range(plan.share):
        strand_ref[b] = states[plan.share - 1 - b]


def running_kernel(strand_ref, offset_ref, running_ref):
    charts = [
        jnp.concatenate([strand_ref[s], offset_ref[s]], axis=0)
        for s in range(offset_ref.shape[0] - 1)
    ]
    for s, chart in enumerate(running(charts)):
        running_ref[s] = chart


def group_kernel(plan, reverse, *refs):
    groups, width = (plan.groups, plan.width)
    parts, (total_ref, before_ref) = (refs[:groups], refs[groups:])
    fixed = []
    for j in range(groups):
        part = parts[j][...]
        fixed.append(jnp.concatenate([part[:width], swapped(part[width:], j, groups)], axis=0))
    me = lax.axis_index("track")
    order = list(range(groups))[::-1] if reverse else list(range(groups))
    charts = [choose(me ^ q, fixed) for q in order]
    place = groups - 1 - me if reverse else me
    befores = [unit_chart(width, plan.rows), charts[0]]
    while len(befores) < groups:
        befores.append(compose(befores[-1], charts[len(befores) - 1]))
    before_ref[...] = choose(place, befores)
    total_ref[...] = joined(charts)


def is_second(mask, reverse):
    second = (lax.axis_index("tm") & mask) != 0
    return jnp.logical_not(second) if reverse else second


def pair_kernel(mask, reverse, own_ref, other_ref, before_ref, joined_ref, after_ref, *half_ref):
    own, other, before = (own_ref[...], other_ref[...], before_ref[...])
    second = is_second(mask, reverse)
    joined = compose(jnp.where(second, other, own), jnp.where(second, own, other))
    joined_ref[...] = joined
    after_ref[...] = jnp.where(second, compose(other, before), before)
    if half_ref:
        rows = joined.shape[0] // 2
        half_ref[0][...] = jnp.where(is_second(1, False), joined[rows:], joined[:rows])


def entering(found, running_ref, stride, reverse):
    before_ref, mine_ref, theirs_ref, half_ref, rest_ref = found
    odd = is_second(1, False)
    mine, theirs, half, rest = (mine_ref[...], theirs_ref[...], half_ref[...], rest_ref[...])
    across = jnp.concatenate([jnp.where(odd, rest, half), jnp.where(odd, half, rest)], axis=0)
    peers = [mine, jnp.where(odd, theirs, mine), jnp.where(odd, mine, theirs), across]
    low, high = (is_second(stride, False), is_second(2 * stride, False))
    quarter = low.astype(jnp.int32) + 2 * high.astype(jnp.int32)
    width = mine.shape[1]
    state = None
    for at in (3, 2, 1) if reverse else (0, 1, 2):
        chart = choose(quarter ^ at, peers)
        ahead = quarter < at if reverse else quarter > at
        if state is None:
            state = jnp.where(ahead, chart[width:], jnp.zeros_like(chart[width:]))
        else:
            state = jnp.where(ahead, apply(state, chart), state)
    state = apply(state, before_ref[...])
    return [state] + [apply(state, running_ref[s]) for s in range(running_ref.shape[0])]


def filter_kernel(plan, stride, *refs):
    found, (running_ref, fpick_ref, gain_ref), refs = (refs[:5], refs[5:8], refs[8:])
    meas, refs = (refs[: plan.groups], refs[plan.groups :])
    strand_ref, bpick_ref, filtered_ref, pushed_ref, offset_ref, total_ref = refs
    states = entering(found, running_ref, stride, False)
    gains = [gain_ref[b : b + 1] for b in range(plan.share)]
    weights = [doubled(fpick_ref[b]) for b in range(plan.share)]
    pushes = {}
    for b, t in plan.forward_steps():
        ahead = times_rows(states[b], weights[b])
        pushes[t] = gains[b] * (step_rows(meas, t) - ahead)
        states[b] = ahead + pushes[t]
        filtered_ref[t] = states[b]
        pushed_ref[t] = pushes[t]
    weights = [doubled(bpick_ref[b]) for b in range(plan.share)]
    states = [None] * plan.share
    for b, t in plan.backward_steps():
        state = pushes[t] if states[b] is None else states[b] + pushes[t]
        states[b] = times_rows(state, weights[b])
    states = states[::-1]
    for b in range(plan.share):
        offset_ref[b] = states[b]
    mats = [strand_ref[b] for b in range(plan.share)]
    while len(states) > 1:
        pairs = range(0, len(states), 2)
        states = [times(states[i], mats[i + 1]) + states[i + 1] for i in pairs]
        mats = [times(mats[i], mats[i + 1]) for i in pairs]
    total_ref[0 : plan.width] = mats[0]
    total_ref[plan.width :] = states[0]


def smooth_kernel(plan, stride, *refs):
    found, (running_ref, picked_ref, filtered_ref, pushed_ref), outs = (refs[:5], refs[5:9], refs[9:])
    tracks = plan.tracks
    states = entering(found, running_ref, stride, True)[::-1]
    weights = [doubled(picked_ref[b]) for b in range(plan.share)]
    for b, t in plan.backward_steps():
        value = filtered_ref[t] + states[b]
        for j in range(plan.groups):
            outs[j][t] = value[j * tracks : (j + 1) * tracks]
        if t % plan.dwell > 0:
            states[b] = times_rows(states[b] + pushed_ref[t], weights[b])


def collect_kernel(plan, *refs):
    parts, out_ref, sem = (refs[: plan.groups], refs[plan.groups], refs[plan.groups + 1])
    copies = []
    for j in range(plan.groups):
        first = pl.multiple_of((lax.axis_index("track") ^ j) * plan.span, plan.span)
        rows = out_ref.at[pl.ds(first, plan.span)]
        copies.append(pltpu.make_async_copy(parts[j], rows, sem.at[j]))
    for copy in copies:
        copy.start()
    for copy in copies:
        copy.wait()


def body(observations, dynamics, smoother_gain, gains, regime):
    length, tracks, width = observations.shape
    blocks = regime.shape[0]
    groups, spans = (lax.axis_size("track"), lax.axis_size("tm"))
    owned = dynamics.shape[0]
    plan = Plan(groups, blocks // groups, length // blocks, owned, tracks, width)
    chart = shape((width + plan.rows, width))
    offset = shape((plan.rows, width))
    half_chart = shape(((width + plan.rows) // 2, width))
    top = spans // 4
    share = plan.share
    block_mats = lambda count: shape((count, width, width), BF16)
    unit = width * width * width
    regime, observations, dynamics, smoother_gain, gains = [
        pltpu.with_memory_space_constraint(value, pltpu.HBM)
        for value in (regime, observations, dynamics, smoother_gain, gains)
    ]

    def swap(value, mask, axis):
        pairs = [(source, source ^ mask) for source in range(lax.axis_size(axis))]
        return lax.ppermute(value, axis, pairs)

    def exchange(values):
        found = [values[0]]
        for j in range(1, groups):
            found.append(swap(values[j], j, "track"))
        return found

    sem = pltpu.SemaphoreType.DMA
    peers = groups - 1
    rows_of = lambda rows: shape((rows, width), BF16)
    further_slots = [rows_of(plan.spare * width)] * peers
    slots = [rows_of(plan.fast * width)] * peers + further_slots
    gained = [rows_of(plan.fast * width + plan.padded)] * peers + further_slots
    own_gain, *trans = call(
        functools.partial(gather_kernel, plan),
        [rows_of(plan.padded)] + gained,
        [SMEM, HBM, VMEM],
        unit,
        [pltpu.VMEM((owned, width), F32), sem],
    )(regime, dynamics, gains)
    atrans = exchange([None, *trans[:peers]])[1:]
    meas = call(
        functools.partial(measured_kernel, plan),
        [shape((plan.span, tracks, width))] * groups,
        [HBM],
        unit,
        [sem((groups,))],
    )(observations)
    meas = exchange(meas)
    over, own, gown, *smooth = call(
        functools.partial(second_gather_kernel, plan),
        [shape((1,), jnp.int32)] + [rows_of(share * width)] * 2 + slots,
        [SMEM, HBM, HBM],
        unit,
        [sem],
        [SMEM] + [VMEM] * (2 + len(slots)),
    )(regime, dynamics, smoother_gain)

    def all_further(values):
        return [swap(value, j % peers + 1, "track") for j, value in enumerate(values)]

    further = lax.cond(
        over[0] > plan.fast, all_further, lambda values: values, [*trans[peers:], *smooth[peers:]]
    )
    squares = lambda count: shape((count, width, width))
    fstrand, ftree, fpick, gain_rows = call(
        functools.partial(forward_kernel, plan),
        [squares(share), squares(share - 1), block_mats(share), shape((share, width))],
        [SMEM] + [VMEM] * (2 * groups),
        300 * unit,
    )(regime, own_gain, own, *atrans, *further[:peers])
    total, foffset = call(
        functools.partial(offset_kernel, plan),
        [chart, shape((share,) + offset.shape)],
        [VMEM] * (4 + groups),
        100 * unit,
    )(fstrand, ftree, fpick, gain_rows, *meas)

    late = smooth[:peers]
    early = (0, 1)
    held, total = lax.optimization_barrier(([late[j] for j in range(peers) if j not in early], total))
    late = [late[j] if j in early else held.pop(0) for j in range(peers)]

    def spread(total):
        return exchange([total] * groups)

    def across(total, reverse):
        maps = spread(total)
        total, before = call(
            functools.partial(group_kernel, plan, reverse),
            [chart, chart],
            [VMEM] * groups,
            20 * unit,
        )(*maps)
        stride = 1
        while 4 * stride < spans:
            last = 8 * stride >= spans
            other = swap(total, stride, "tm")
            total, before, *half = call(
                functools.partial(pair_kernel, stride, reverse),
                [chart, chart] + [half_chart] * last,
                [VMEM] * 3,
                20 * unit,
            )(total, other, before)
            stride *= 2
        near = [(at, at ^ (stride << (at & 1))) for at in range(spans)]
        mine = lax.ppermute(total, "tm", near)
        half = swap(half[0], 3 * stride, "tm")
        theirs = swap(mine, 1, "tm")
        return before, mine, theirs, half, swap(half, 1, "tm")

    for j, value in enumerate(late):
        late[j] = swap(value, j + 1, "track")
    bstrand, bpick = call(
        functools.partial(backward_kernel, plan),
        [shape((share, width, width)), block_mats(share)],
        [SMEM] + [VMEM] * (2 * groups - 1),
        300 * unit,
    )(regime, gown, *late, *further[peers:])

    found = across(total, False)
    runs = [shape((share - 1,) + chart.shape)]
    (frun,) = call(running_kernel, runs, [VMEM] * 2, 60 * unit)(fstrand, foffset)
    filtered, pushed, offsets, total = call(
        functools.partial(filter_kernel, plan, top),
        [shape((plan.span, plan.rows, width))] * 2 + [shape((share,) + offset.shape), chart],
        [VMEM] * (10 + groups),
        100 * unit,
    )(*found, frun, fpick, gain_rows, *meas, bstrand, bpick)

    found = across(total, True)
    (brun,) = call(running_kernel, runs, [VMEM] * 2, 60 * unit)(bstrand, offsets)
    outs = call(
        functools.partial(smooth_kernel, plan, top),
        [shape((plan.span, tracks, width))] * groups,
        [VMEM] * 9,
        50 * unit,
    )(*found, brun, bpick, filtered, pushed)
    sent = exchange(outs)
    return call(
        functools.partial(collect_kernel, plan),
        [shape((length, tracks, width))],
        [VMEM] * groups,
        unit,
        [sem((groups,))],
        [HBM],
    )(*sent)[0]


def solution(mesh):
    placed = (
        P("tm", "track", None),
        P("track", None, None),
        P("track", None, None),
        P("track", None),
        P("tm"),
    )

    return jax.shard_map(
        body, mesh=mesh, in_specs=placed, out_specs=P("tm", "track", None), check_vma=False
    )
```

```python
import functools

import jax
import jax.numpy as jnp
from jax import lax
from jax.experimental import pallas as pl
from jax.experimental.pallas import tpu as pltpu
from jax.sharding import PartitionSpec as P


F32 = jnp.float32
BF16 = jnp.bfloat16
VMEM = pl.BlockSpec(memory_space=pltpu.VMEM)
SMEM = pl.BlockSpec(memory_space=pltpu.SMEM)
HBM = pl.BlockSpec(memory_space=pltpu.HBM)
GRANT = 16 * 1024 * 1024


def call(kernel, outs, ins, cost, scratch=(), places=None):
    return pl.pallas_call(
        kernel,
        out_shape=outs,
        in_specs=ins,
        out_specs=places or [VMEM] * len(outs),
        scratch_shapes=list(scratch),
        compiler_params=pltpu.CompilerParams(vmem_limit_bytes=GRANT),
        cost_estimate=pl.CostEstimate(flops=cost, bytes_accessed=cost // 64, transcendentals=0),
    )


def shape(dims, dtype=F32):
    return jax.ShapeDtypeStruct(dims, dtype)


def split(value):
    high = value.astype(BF16)
    low = (value - high.astype(F32)).astype(BF16)
    return high, low


def times_rows(value, doubled):
    pieces = jnp.concatenate(split(value), axis=1)
    return lax.dot_general(
        pieces, doubled, (((1,), (1,)), ((), ())), preferred_element_type=F32
    )


def times(value, matrix):
    high, low = split(value)
    upper, lower = split(matrix)
    left = jnp.concatenate([high, low, high], axis=1)
    right = jnp.concatenate([upper, upper, lower], axis=0)
    return jnp.dot(left, right, preferred_element_type=F32)


def compose(first, second):
    width = first.shape[1]
    product = times(first, second[:width])
    return jnp.concatenate([product[:width], product[width:] + second[width:]], axis=0)


def apply(state, chart):
    width = chart.shape[1]
    return times(state, chart[:width]) + chart[width:]


def unit_matrix(width):
    rows = lax.broadcasted_iota(jnp.int32, (width, width), 0)
    return (rows == lax.broadcasted_iota(jnp.int32, (width, width), 1)).astype(F32)


def unit_chart(width, rows):
    return jnp.concatenate([unit_matrix(width), jnp.zeros((rows, width), F32)], axis=0)


def choose(index, options):
    value = options[0]
    for j in range(1, len(options)):
        value = jnp.where(index == j, options[j], value)
    return value


def swapped(rows, mask, groups):
    block = rows.shape[0] // groups
    return jnp.concatenate(
        [rows[(j ^ mask) * block : ((j ^ mask) + 1) * block] for j in range(groups)], axis=0
    )


def doubled(matrix):
    return jnp.concatenate([matrix, matrix], axis=1)


def step_rows(parts, t):
    return jnp.concatenate([part[t] for part in parts], axis=0)


class Plan:
    def __init__(self, groups, share, dwell, owned, tracks, width):
        self.groups, self.share, self.dwell = groups, share, dwell
        self.owned, self.tracks, self.width = owned, tracks, width
        self.span, self.rows = share * dwell, groups * tracks
        self.padded = -(-share // 16) * 16
        self.spare = share // 4
        self.fast = share - self.spare

    def local(self, regime_ref, peer, b):
        return regime_ref[peer * self.share + b] - lax.axis_index("track") * self.owned

    def here(self, regime_ref, peer, b):
        return jnp.clip(self.local(regime_ref, peer, b), 0, self.owned - 1)

    def source(self, regime_ref, b):
        me = lax.axis_index("track")
        return (regime_ref[me * self.share + b] // self.owned) ^ me

    def forward_steps(self):
        return [(b, b * self.dwell + i) for i in range(self.dwell) for b in range(self.share)]

    def backward_steps(self):
        turn = self.dwell - 1
        return [(b, t + turn - 2 * (t % self.dwell)) for b, t in self.forward_steps()]


def block_of(plan, ref, at):
    return ref.at[pl.ds(pl.multiple_of(at * plan.width, plan.width), plan.width)]


def start_rows(plan, regime_ref, table_ref, targets, sem):
    def row(held, at, target):
        @pl.when(held)
        def _():
            pltpu.make_async_copy(table_ref.at[at], target, sem).start()

    count = jnp.int32(0)
    for j, main, more in targets:
        peer = lax.axis_index("track") ^ j
        slot = jnp.int32(0)
        for b in range(plan.share):
            at = plan.local(regime_ref, peer, b)
            held = jnp.logical_and(at >= 0, at < plan.owned)
            at = jnp.clip(at, 0, plan.owned - 1)
            count = count + held.astype(jnp.int32)
            if j == 0:
                row(held, at, block_of(plan, main, b))
                continue
            if b < plan.fast:
                row(held, at, block_of(plan, main, slot))
            else:
                fits = slot < plan.fast
                room = jnp.minimum(slot, plan.fast - 1)
                row(jnp.logical_and(held, fits), at, block_of(plan, main, room))
                late = jnp.clip(slot - plan.fast, 0, plan.spare - 1)
                row(jnp.logical_and(held, jnp.logical_not(fits)), at, block_of(plan, more, late))
            slot = slot + held.astype(jnp.int32)
    return count


def await_rows(plan, table_ref, target_ref, sem, count):
    def one(_, carry):
        pltpu.make_async_copy(table_ref.at[0], block_of(plan, target_ref, 0), sem).wait()
        return carry

    lax.fori_loop(0, count, one, 0)


def remote_targets(plan, refs):
    peers = plan.groups - 1
    return [(j + 1, refs[j], refs[peers + j]) for j in range(peers)]


def gather_kernel(plan, regime_ref, table_ref, gains_ref, *refs):
    own_ref, refs, (gain_ref, sem) = (refs[0], refs[1:-2], refs[-2:])
    count = start_rows(plan, regime_ref, table_ref, remote_targets(plan, refs), sem)
    gain_ref[...] = gains_ref[...].astype(F32)
    for j in range(plan.groups):
        peer = lax.axis_index("track") ^ j
        rows = [min(b, plan.share - 1) for b in range(plan.padded)]
        found = [gain_ref[pl.ds(plan.here(regime_ref, peer, b), 1), :] for b in range(plan.share)]
        tile = jnp.concatenate([found[b] for b in rows], axis=0).astype(BF16)
        if j:
            refs[j - 1][plan.fast * plan.width :] = tile
        else:
            own_ref[...] = tile
    await_rows(plan, table_ref, refs[0], sem, count)


def second_gather_kernel(plan, regime_ref, first_ref, second_ref, *refs):
    over_ref, own_first, own_second, refs, sem = (*refs[:3], refs[3:-1], refs[-1])
    targets = [(0, own_second, None)] + remote_targets(plan, refs)
    count = start_rows(plan, regime_ref, first_ref, [(0, own_first, None)], sem)
    count = count + start_rows(plan, regime_ref, second_ref, targets, sem)
    over_ref[0] = most_slots(plan, regime_ref)
    await_rows(plan, first_ref, own_first, sem, count)


def picked_matrix(plan, regime_ref, refs, b):
    peers = plan.groups - 1
    own, main, more = (refs[0], refs[1 : peers + 1], refs[peers + 1 :])
    me = lax.axis_index("track")
    holder = [lax.div(regime_ref[me * plan.share + i], plan.owned) for i in range(b + 1)]
    slot = sum((holder[i] == holder[b]).astype(jnp.int32) for i in range(b)) if b else 0
    source = holder[b] ^ me
    mine = own[b * plan.width : (b + 1) * plan.width]
    if b < plan.fast:
        return choose(source, [mine] + [block_of(plan, part, slot)[...] for part in main])
    room = jnp.minimum(slot, plan.fast - 1)
    found = choose(source, [mine] + [block_of(plan, part, room)[...] for part in main])
    late = jnp.clip(slot - plan.fast, 0, plan.spare - 1)
    rest = choose(source, [mine] + [block_of(plan, part, late)[...] for part in more])
    return jnp.where(slot < plan.fast, found, rest)


def measured_kernel(plan, obs_ref, *refs):
    meas, sem = (refs[:-1], refs[-1])
    copies = []
    for j in range(plan.groups):
        first = pl.multiple_of((lax.axis_index("track") ^ j) * plan.span, plan.span)
        rows = obs_ref.at[pl.ds(first, plan.span)]
        copies.append(pltpu.make_async_copy(rows, meas[j], sem.at[j]))
    for copy in copies:
        copy.start()
    for copy in copies:
        copy.wait()


def most_slots(plan, regime_ref):
    most = jnp.int32(0)
    for peer in range(plan.groups):
        holder = [lax.div(regime_ref[peer * plan.share + b], plan.owned) for b in range(plan.share)]
        for q in range(plan.groups):
            if q != peer:
                most = jnp.maximum(most, sum((at == q).astype(jnp.int32) for at in holder))
    return most


def joined(charts):
    while len(charts) > 1:
        odd = charts[len(charts) // 2 * 2 :]
        charts = [compose(charts[i], charts[i + 1]) for i in range(0, len(charts) - 1, 2)] + odd
    return charts[0]


def running(charts):
    if len(charts) == 1:
        return charts
    pairs = running([compose(charts[i], charts[i + 1]) for i in range(0, len(charts) - 1, 2)])
    found = [charts[0]]
    for i in range(1, len(charts)):
        found.append(pairs[i // 2] if i % 2 else compose(pairs[i // 2 - 1], charts[i]))
    return found


def forward_kernel(plan, regime_ref, own_gain_ref, *refs):
    mats, (strand_ref, tree_ref, picked_ref, gain_ref) = (refs[:-4], refs[-4:])
    tiles = [own_gain_ref[...].astype(F32)]
    tiles += [part[plan.fast * plan.width :].astype(F32) for part in mats[1 : plan.groups]]
    weights, gains, states = ([], [], [])
    for b in range(plan.share):
        picked = picked_matrix(plan, regime_ref, mats, b)
        picked_ref[b] = picked
        weights.append(doubled(picked))
        source = plan.source(regime_ref, b)
        gains.append(choose(source, [tile[b : b + 1] for tile in tiles]))
        gain_ref[b : b + 1] = gains[b]
        states.append(picked.astype(F32).T * (1.0 - gains[b]))
    for b, t in plan.forward_steps():
        if t % plan.dwell > 0:
            states[b] = times_rows(states[b], weights[b]) * (1.0 - gains[b])
    for b in range(plan.share):
        strand_ref[b] = states[b]
    at = 0
    while len(states) > 1:
        states = [times(states[i], states[i + 1]) for i in range(0, len(states), 2)]
        for state in states:
            tree_ref[at] = state
            at += 1


def offset_kernel(plan, strand_ref, tree_ref, picked_ref, gain_ref, *refs):
    meas, (total_ref, offset_ref) = (refs[:-2], refs[-2:])
    gains = [gain_ref[b : b + 1] for b in range(plan.share)]
    weights = [doubled(picked_ref[b]) for b in range(plan.share)]
    states = [gains[b] * step_rows(meas, b * plan.dwell) for b in range(plan.share)]
    for b, t in plan.forward_steps():
        if t % plan.dwell > 0:
            moved = times_rows(states[b], weights[b]) * (1.0 - gains[b])
            states[b] = moved + gains[b] * step_rows(meas, t)
    for b in range(plan.share):
        offset_ref[b] = states[b]
    mats = [strand_ref[b] for b in range(plan.share)]
    at = 0
    while len(states) > 1:
        pairs = range(0, len(states), 2)
        states = [times(states[i], mats[i + 1]) + states[i + 1] for i in pairs]
        mats = [tree_ref[at + i] for i in range(len(states))]
        at += len(states)
    total_ref[: plan.width] = mats[0]
    total_ref[plan.width :] = states[0]


def backward_kernel(plan, regime_ref, *refs):
    mats, (strand_ref, picked_ref) = (refs[:-2], refs[-2:])
    weights, states = ([], [])
    for b in range(plan.share):
        picked = picked_matrix(plan, regime_ref, mats, b)
        picked_ref[b] = picked
        weights.append(doubled(picked))
        states.append(picked.astype(F32).T)
    for b, t in plan.backward_steps():
        if t % plan.dwell < plan.dwell - 1:
            states[b] = times_rows(states[b], weights[b])
    for b in range(plan.share):
        strand_ref[b] = states[plan.share - 1 - b]


def running_kernel(strand_ref, offset_ref, running_ref):
    charts = [
        jnp.concatenate([strand_ref[s], offset_ref[s]], axis=0)
        for s in range(offset_ref.shape[0] - 1)
    ]
    for s, chart in enumerate(running(charts)):
        running_ref[s] = chart


def group_kernel(plan, reverse, *refs):
    groups, width = (plan.groups, plan.width)
    parts, (total_ref, before_ref) = (refs[:groups], refs[groups:])
    fixed = []
    for j in range(groups):
        part = parts[j][...]
        fixed.append(jnp.concatenate([part[:width], swapped(part[width:], j, groups)], axis=0))
    me = lax.axis_index("track")
    order = list(range(groups))[::-1] if reverse else list(range(groups))
    charts = [choose(me ^ q, fixed) for q in order]
    place = groups - 1 - me if reverse else me
    befores = [unit_chart(width, plan.rows), charts[0]]
    while len(befores) < groups:
        befores.append(compose(befores[-1], charts[len(befores) - 1]))
    before_ref[...] = choose(place, befores)
    total_ref[...] = joined(charts)


def is_second(mask, reverse):
    second = (lax.axis_index("tm") & mask) != 0
    return jnp.logical_not(second) if reverse else second


def pair_kernel(mask, reverse, own_ref, other_ref, before_ref, joined_ref, after_ref, *half_ref):
    own, other, before = (own_ref[...], other_ref[...], before_ref[...])
    second = is_second(mask, reverse)
    joined = compose(jnp.where(second, other, own), jnp.where(second, own, other))
    joined_ref[...] = joined
    after_ref[...] = jnp.where(second, compose(other, before), before)
    if half_ref:
        rows = joined.shape[0] // 2
        half_ref[0][...] = jnp.where(is_second(1, False), joined[rows:], joined[:rows])


def entering(found, running_ref, stride, reverse):
    before_ref, mine_ref, theirs_ref, half_ref, rest_ref = found
    odd = is_second(1, False)
    mine, theirs, half, rest = (mine_ref[...], theirs_ref[...], half_ref[...], rest_ref[...])
    across = jnp.concatenate([jnp.where(odd, rest, half), jnp.where(odd, half, rest)], axis=0)
    peers = [mine, jnp.where(odd, theirs, mine), jnp.where(odd, mine, theirs), across]
    low, high = (is_second(stride, False), is_second(2 * stride, False))
    quarter = low.astype(jnp.int32) + 2 * high.astype(jnp.int32)
    width = mine.shape[1]
    state = None
    for at in (3, 2, 1) if reverse else (0, 1, 2):
        chart = choose(quarter ^ at, peers)
        ahead = quarter < at if reverse else quarter > at
        if state is None:
            state = jnp.where(ahead, chart[width:], jnp.zeros_like(chart[width:]))
        else:
            state = jnp.where(ahead, apply(state, chart), state)
    state = apply(state, before_ref[...])
    return [state] + [apply(state, running_ref[s]) for s in range(running_ref.shape[0])]


def filter_kernel(plan, stride, *refs):
    found, (running_ref, fpick_ref, gain_ref), refs = (refs[:5], refs[5:8], refs[8:])
    meas, refs = (refs[: plan.groups], refs[plan.groups :])
    strand_ref, bpick_ref, filtered_ref, pushed_ref, offset_ref, total_ref = refs
    states = entering(found, running_ref, stride, False)
    gains = [gain_ref[b : b + 1] for b in range(plan.share)]
    weights = [doubled(fpick_ref[b]) for b in range(plan.share)]
    pushes = {}
    for b, t in plan.forward_steps():
        ahead = times_rows(states[b], weights[b])
        pushes[t] = gains[b] * (step_rows(meas, t) - ahead)
        states[b] = ahead + pushes[t]
        filtered_ref[t] = states[b]
        pushed_ref[t] = pushes[t]
    weights = [doubled(bpick_ref[b]) for b in range(plan.share)]
    states = [None] * plan.share
    for b, t in plan.backward_steps():
        state = pushes[t] if states[b] is None else states[b] + pushes[t]
        states[b] = times_rows(state, weights[b])
    states = states[::-1]
    for b in range(plan.share):
        offset_ref[b] = states[b]
    mats = [strand_ref[b] for b in range(plan.share)]
    while len(states) > 1:
        pairs = range(0, len(states), 2)
        states = [times(states[i], mats[i + 1]) + states[i + 1] for i in pairs]
        mats = [times(mats[i], mats[i + 1]) for i in pairs]
    total_ref[0 : plan.width] = mats[0]
    total_ref[plan.width :] = states[0]


def smooth_kernel(plan, stride, *refs):
    found, (running_ref, picked_ref, filtered_ref, pushed_ref), outs = (refs[:5], refs[5:9], refs[9:])
    tracks = plan.tracks
    states = entering(found, running_ref, stride, True)[::-1]
    weights = [doubled(picked_ref[b]) for b in range(plan.share)]
    for b, t in plan.backward_steps():
        value = filtered_ref[t] + states[b]
        for j in range(plan.groups):
            outs[j][t] = value[j * tracks : (j + 1) * tracks]
        if t % plan.dwell > 0:
            states[b] = times_rows(states[b] + pushed_ref[t], weights[b])


def collect_kernel(plan, *refs):
    parts, out_ref, sem = (refs[: plan.groups], refs[plan.groups], refs[plan.groups + 1])
    copies = []
    for j in range(plan.groups):
        first = pl.multiple_of((lax.axis_index("track") ^ j) * plan.span, plan.span)
        rows = out_ref.at[pl.ds(first, plan.span)]
        copies.append(pltpu.make_async_copy(parts[j], rows, sem.at[j]))
    for copy in copies:
        copy.start()
    for copy in copies:
        copy.wait()


def body(observations, dynamics, smoother_gain, gains, regime):
    length, tracks, width = observations.shape
    blocks = regime.shape[0]
    groups, spans = (lax.axis_size("track"), lax.axis_size("tm"))
    owned = dynamics.shape[0]
    plan = Plan(groups, blocks // groups, length // blocks, owned, tracks, width)
    chart = shape((width + plan.rows, width))
    offset = shape((plan.rows, width))
    half_chart = shape(((width + plan.rows) // 2, width))
    top = spans // 4
    share = plan.share
    block_mats = lambda count: shape((count, width, width), BF16)
    unit = width * width * width
    regime, observations, dynamics, smoother_gain, gains = [
        pltpu.with_memory_space_constraint(value, pltpu.HBM)
        for value in (regime, observations, dynamics, smoother_gain, gains)
    ]

    def swap(value, mask, axis):
        pairs = [(source, source ^ mask) for source in range(lax.axis_size(axis))]
        return lax.ppermute(value, axis, pairs)

    def exchange(values):
        found = [values[0]]
        for j in range(1, groups):
            found.append(swap(values[j], j, "track"))
        return found

    sem = pltpu.SemaphoreType.DMA
    peers = groups - 1
    rows_of = lambda rows: shape((rows, width), BF16)
    further_slots = [rows_of(plan.spare * width)] * peers
    slots = [rows_of(plan.fast * width)] * peers + further_slots
    gained = [rows_of(plan.fast * width + plan.padded)] * peers + further_slots
    own_gain, *trans = call(
        functools.partial(gather_kernel, plan),
        [rows_of(plan.padded)] + gained,
        [SMEM, HBM, VMEM],
        unit,
        [pltpu.VMEM((owned, width), F32), sem],
    )(regime, dynamics, gains)
    atrans = exchange([None, *trans[:peers]])[1:]
    meas = call(
        functools.partial(measured_kernel, plan),
        [shape((plan.span, tracks, width))] * groups,
        [HBM],
        unit,
        [sem((groups,))],
    )(observations)
    meas = exchange(meas)
    over, own, gown, *smooth = call(
        functools.partial(second_gather_kernel, plan),
        [shape((1,), jnp.int32)] + [rows_of(share * width)] * 2 + slots,
        [SMEM, HBM, HBM],
        unit,
        [sem],
        [SMEM] + [VMEM] * (2 + len(slots)),
    )(regime, dynamics, smoother_gain)

    def all_further(values):
        return [swap(value, j % peers + 1, "track") for j, value in enumerate(values)]

    further = lax.cond(
        over[0] > plan.fast, all_further, lambda values: values, [*trans[peers:], *smooth[peers:]]
    )
    squares = lambda count: shape((count, width, width))
    fstrand, ftree, fpick, gain_rows = call(
        functools.partial(forward_kernel, plan),
        [squares(share), squares(share - 1), block_mats(share), shape((share, width))],
        [SMEM] + [VMEM] * (2 * groups),
        300 * unit,
    )(regime, own_gain, own, *atrans, *further[:peers])
    total, foffset = call(
        functools.partial(offset_kernel, plan),
        [chart, shape((share,) + offset.shape)],
        [VMEM] * (4 + groups),
        100 * unit,
    )(fstrand, ftree, fpick, gain_rows, *meas)

    late = smooth[:peers]
    early = (0, 1)
    held, total = lax.optimization_barrier(([late[j] for j in range(peers) if j not in early], total))
    late = [late[j] if j in early else held.pop(0) for j in range(peers)]

    def spread(total):
        return exchange([total] * groups)

    def across(total, reverse):
        maps = spread(total)
        total, before = call(
            functools.partial(group_kernel, plan, reverse),
            [chart, chart],
            [VMEM] * groups,
            20 * unit,
        )(*maps)
        stride = 1
        while 4 * stride < spans:
            last = 8 * stride >= spans
            other = swap(total, stride, "tm")
            total, before, *half = call(
                functools.partial(pair_kernel, stride, reverse),
                [chart, chart] + [half_chart] * last,
                [VMEM] * 3,
                20 * unit,
            )(total, other, before)
            stride *= 2
        near = [(at, at ^ (stride << (at & 1))) for at in range(spans)]
        mine = lax.ppermute(total, "tm", near)
        half = swap(half[0], 3 * stride, "tm")
        theirs = swap(mine, 1, "tm")
        return before, mine, theirs, half, swap(half, 1, "tm")

    for j, value in enumerate(late):
        late[j] = swap(value, j + 1, "track")
    bstrand, bpick = call(
        functools.partial(backward_kernel, plan),
        [shape((share, width, width)), block_mats(share)],
        [SMEM] + [VMEM] * (2 * groups - 1),
        300 * unit,
    )(regime, gown, *late, *further[peers:])

    found = across(total, False)
    runs = [shape((share - 1,) + chart.shape)]
    (frun,) = call(running_kernel, runs, [VMEM] * 2, 60 * unit)(fstrand, foffset)
    filtered, pushed, offsets, total = call(
        functools.partial(filter_kernel, plan, top),
        [shape((plan.span, plan.rows, width))] * 2 + [shape((share,) + offset.shape), chart],
        [VMEM] * (10 + groups),
        100 * unit,
    )(*found, frun, fpick, gain_rows, *meas, bstrand, bpick)

    found = across(total, True)
    (brun,) = call(running_kernel, runs, [VMEM] * 2, 60 * unit)(bstrand, offsets)
    outs = call(
        functools.partial(smooth_kernel, plan, top),
        [shape((plan.span, tracks, width))] * groups,
        [VMEM] * 9,
        50 * unit,
    )(*found, brun, bpick, filtered, pushed)
    sent = exchange(outs)
    return call(
        functools.partial(collect_kernel, plan),
        [shape((length, tracks, width))],
        [VMEM] * groups,
        unit,
        [sem((groups,))],
        [HBM],
    )(*sent)[0]


def solution(mesh):
    placed = (
        P("tm", "track", None),
        P("track", None, None),
        P("track", None, None),
        P("track", None),
        P("tm"),
    )

    return jax.shard_map(
        body, mesh=mesh, in_specs=placed, out_specs=P("tm", "track", None), check_vma=False
    )
```
